256 devices in a mesh: wide: 32 (over z, x_lo, core), tm: 8 (over x_hi, y).
Axes of the slice: x: 4 (x_hi: 2, x_lo: 2; x = x_hi * 2 + x_lo), y: 4, z: 8, core: 2. Of those that a mesh axis runs over, the one named last changes fastest.
Arguments:
- clips_in: bfloat16 [32, 32, 14, 14, 256], P('wide', 'tm'), may hold values from -6 to 6
- w_spatial: bfloat16 [3, 3, 256, 256], replicated, may hold values from -0.125 to 0.125
- w_temporal: bfloat16 [3, 256, 256], replicated, may hold values from -0.21875 to 0.21875
- w_proj: bfloat16 [256, 512], replicated, may hold values from -0.375 to 0.375
- prompts: bfloat16 [4096, 512], P('tm'), may hold values from -6 to 6
- positives: int32 [32, 4], P('wide'), may hold values from 0 to 4095
Outputs:
- grad_spatial: float32 [3, 3, 256, 256], replicated
- grad_temporal: float32 [3, 256, 256], replicated
- grad_proj: float32 [256, 512], replicated
- grad_prompts: float32 [4096, 512], P('tm')
The draws below stay inside these ranges and needn't reach their ends.
Inputs may be any that keep to these rules, and one draw needn't show every extreme that they name: `positives`: 4 positive prompt ids for each clip; a clip may name one id more than once.
All inputs are finite; a program needn't handle non-finite values.
Results may differ from the reference program's by a relative error of at most 0.0037.
Values may be sent and summed in bfloat16 or wider, within the bound.
A program may use at most 64 MiB of HBM per device.

```python
import jax
import jax.numpy as jnp
from jax import lax

C = 256
E = 512
P_SIZE = 4096
K = 4
SIDE = 14
FRAMES = 32
CLIPS = 32


def touch_ends(array, own_key, low, largest):
    index_at = [jax.random.randint(jax.random.fold_in(own_key, axis), (), 0, length) for axis, length in enumerate(array.shape)]
    widest = array.shape.index(max(array.shape))
    next_to = index_at[:widest] + [(index_at[widest] + 1) % array.shape[widest]] + index_at[widest + 1:]
    return array.at[tuple(index_at)].set(low).at[tuple(next_to)].set(largest)


def level_of(stream_key, dims, pieces, smallest, high):
    factor_of, own = 1.0, jax.random.fold_in(stream_key, 6)
    for axis_at, shards_of in pieces:
        steps = jnp.exp(jax.random.uniform(jax.random.fold_in(own, axis_at), (shards_of,), jnp.float32, smallest / len(pieces), high / len(pieces)))
        factor_of = factor_of * jnp.repeat(steps, dims[axis_at] // shards_of).reshape([-1 if axis == axis_at else 1 for axis in range(len(dims))])
    return factor_of


def scatter_about(own_key, dims, scale, reach, cuts=(), kind=jnp.bfloat16):
    entries = jax.random.normal(own_key, dims, jnp.float32) * scale
    if len(cuts) > 0:
        entries = level_of(own_key, dims, cuts, -0.22, 0.18) * entries
    return jnp.clip(entries, min=-reach, max=reach).astype(kind)


def setup_inputs(seed: int = 0) -> dict:
    splits = jax.random.split(jax.random.key(seed), 7)
    clips_in = scatter_about(splits[0], (CLIPS, FRAMES, SIDE, SIDE, C), 1.0, 6.0, ((0, 32), (1, 8)))
    w_spatial = scatter_about(splits[1], (3, 3, C, C), (9 * C) ** -0.5, 0.125)
    w_temporal = scatter_about(splits[2], (3, C, C), (3 * C) ** -0.5, 0.21875)
    w_proj = scatter_about(splits[3], (C, E), C ** -0.5, 0.375)
    prompts = scatter_about(splits[4], (P_SIZE, E), 1.0, 6.0, ((0, 8),))
    positives = touch_ends(jax.random.randint(splits[5], (CLIPS, K), 0, P_SIZE), jax.random.fold_in(splits[5], 1), 0, P_SIZE - 1).astype(jnp.int32)
    return dict(clips_in=clips_in, w_spatial=w_spatial, w_temporal=w_temporal, w_proj=w_proj, prompts=prompts, positives=positives)


HI = lax.Precision.HIGHEST

def dsilu(v):
    sig = jax.nn.sigmoid(v)
    return sig * (1.0 + v * (1.0 - sig))

def clip_forward(frames_in, w_spatial, w_temporal):
    count = frames_in.shape[0]
    rows = count * SIDE * SIDE
    padded = jnp.pad(frames_in, ((0, 0), (1, 1), (1, 1), (0, 0)))
    pre_s = jnp.zeros((rows, C), jnp.float32)
    for a in range(3):
        for b in range(3):
            window = padded[:, a:a + SIDE, b:b + SIDE, :].reshape(rows, C)
            pre_s = pre_s + jnp.dot(window, w_spatial[a, b], preferred_element_type=jnp.float32)
    act = jax.nn.silu(pre_s).astype(jnp.bfloat16).reshape(count, SIDE, SIDE, C)
    act_pad = jnp.pad(act, ((1, 1), (0, 0), (0, 0), (0, 0)))
    pre_t = jnp.zeros((rows, C), jnp.float32)
    for t in range(3):
        pre_t = pre_t + jnp.dot(act_pad[t:t + count].reshape(rows, C), w_temporal[t], preferred_element_type=jnp.float32)
    out = frames_in.reshape(rows, C).astype(jnp.float32) + jax.nn.silu(pre_t)
    return (padded, pre_s, act_pad, pre_t, lax.optimization_barrier(jnp.sum(out, axis=0)))

def contract(left, right):
    return lax.dot_general(left, right, (((0,), (0,)), ((), ())), preferred_element_type=jnp.float32)

def reference(clips_in, w_spatial, w_temporal, w_proj, prompts, positives):
    pooled = lax.map(lambda one: clip_forward(one, w_spatial, w_temporal)[4], clips_in)
    z = jnp.dot(pooled, w_proj.astype(jnp.float32), precision=HI)
    znorm = jnp.sqrt(lax.optimization_barrier(jnp.sum(z * z, axis=1, keepdims=True)) + 1e-06)
    zhat = z / znorm
    p32 = prompts.astype(jnp.float32)
    pnorm = jnp.sqrt(lax.optimization_barrier(jnp.sum(p32 * p32, axis=1, keepdims=True)) + 1e-06)
    phat = p32 / pnorm
    scores = 16.0 * jnp.dot(zhat, phat.T, precision=HI)
    expo = jnp.exp(scores)
    ids = jnp.arange(P_SIZE, dtype=jnp.int32)
    multi = lax.optimization_barrier(jnp.sum((positives[:, :, None] == ids[None, None, :]).astype(jnp.float32), axis=1))
    total = lax.optimization_barrier(jnp.sum(expo, axis=1, keepdims=True))
    pos_total = lax.optimization_barrier(jnp.sum(multi * expo, axis=1, keepdims=True))
    g_s = expo / total - multi * expo / pos_total
    g_phat = 16.0 * jnp.dot(g_s.T, zhat, precision=HI)
    grad_prompts = (g_phat - phat * lax.optimization_barrier(jnp.sum(phat * g_phat, axis=1, keepdims=True))) / pnorm
    g_zhat = 16.0 * jnp.dot(g_s, phat, precision=HI)
    g_z = (g_zhat - zhat * lax.optimization_barrier(jnp.sum(zhat * g_zhat, axis=1, keepdims=True))) / znorm
    grad_proj = jnp.dot(pooled.T, g_z, precision=HI)
    g_pooled = jnp.dot(g_z, w_proj.astype(jnp.float32).T, precision=HI)

    def backward(carry, item):
        frames_in, g_one = item
        count = frames_in.shape[0]
        rows = count * SIDE * SIDE
        padded, pre_s, act_pad, pre_t, unused = clip_forward(frames_in, w_spatial, w_temporal)
        g_t = (g_one[None, :] * dsilu(pre_t)).astype(jnp.bfloat16)
        g_temporal = jnp.stack([contract(act_pad[t:t + count].reshape(rows, C), g_t) for t in range(3)])
        g_pad = jnp.pad(g_t.reshape(count, SIDE, SIDE, C), ((1, 1), (0, 0), (0, 0), (0, 0)))
        g_act = jnp.zeros((rows, C), jnp.float32)
        for t in range(3):
            g_act = g_act + jnp.dot(g_pad[2 - t:2 - t + count].reshape(rows, C), w_temporal[t].T, preferred_element_type=jnp.float32)
        g_sp = (g_act * dsilu(pre_s)).astype(jnp.bfloat16)
        g_spatial = jnp.stack([jnp.stack([contract(padded[:, a:a + SIDE, b:b + SIDE, :].reshape(rows, C), g_sp) for b in range(3)]) for a in range(3)])
        return ((carry[0] + g_spatial, carry[1] + g_temporal), None)
    init = (jnp.zeros((3, 3, C, C), jnp.float32), jnp.zeros((3, C, C), jnp.float32))
    sums, unused = lax.scan(backward, init, (clips_in, g_pooled))
    return (sums[0], sums[1], grad_proj, grad_prompts)
```

```python
import functools

import jax
import jax.numpy as jnp
from jax import lax
from jax.experimental import pallas as pl
from jax.experimental.pallas import tpu as pltpu
from jax.sharding import PartitionSpec as P

MESH = pl.DeviceIdType.MESH
F32 = jnp.float32
BF16 = jnp.bfloat16
HI = lax.Precision.HIGHEST

X_LO = 2
X_HI = 2
CORES = 2
LINE = 16

HALO, DHALO, POOL, AB, HEAD, PAIR, ZHEAD, CORE, XY, ZSUM, ZALL, XYALL, COREALL, SEMS = (
    0, 2, 4, 5, 6, 7, 8, 9, 13, 17, 18, 19, 23, 27
)


def dot(left, right):
    return jnp.dot(left, right, preferred_element_type=F32)


def sigmoid(v):
    return 1.0 / (1.0 + jnp.exp(-v))


def dsilu(v):
    sig = sigmoid(v)
    return sig * (1.0 + v * (1.0 - sig))


def same(n):
    return lax.broadcasted_iota(jnp.int32, (n, n), 0) == lax.broadcasted_iota(jnp.int32, (n, n), 1)


def to_column(row):
    return jnp.sum(jnp.where(same(row.shape[1]), row, 0.0), axis=1, keepdims=True)


def to_row(column):
    return jnp.sum(jnp.where(same(column.shape[0]), column, 0.0), axis=0, keepdims=True)


def step_kernel(
    sizes,
    x_ref, ws_ref, wt_ref, wp_ref, pr_ref, pos_ref,
    ag_ref, gproj_ref, gprm_ref,
    xs_ref, pre_ref, act_ref, dt_ref, dsend_ref, dhalo_ref, gt_ref, gs_ref, xt_ref, actt_ref, wtt_ref,
    ph_ref, pool_ref, ab_ref, wg_ref, gbuf_ref, rbuf_ref, cs_ref, xyr_ref, zsrc_ref, zr_ref, zred_ref, zg_ref,
    snd, rcv,
):
    n_wide, n_tm, frames, side, chan, embed, shard = sizes
    rows = side * LINE
    n_z = n_wide // (X_LO * CORES)
    n_y = n_tm // X_HI
    n_x = X_HI * X_LO
    n_xy = n_x * n_y

    wide = lax.axis_index("wide")
    tm = lax.axis_index("tm")
    core = wide % CORES
    x_lo = (wide // CORES) % X_LO
    z = wide // (CORES * X_LO)
    y = tm % n_y
    x = (tm // n_y) * X_LO + x_lo
    mine = x * n_y + y

    def xy_partner(d):
        px = (x + d // n_y) % n_x
        py = (y + d % n_y) % n_y
        return px * n_y + py, (z * (CORES * X_LO) + (px % X_LO) * CORES + core, (px // X_LO) * n_y + py)

    def z_partner(d):
        pz = (z + d) % n_z
        return pz, (pz * (CORES * X_LO) + x_lo * CORES + core, tm)

    sibling = (wide + 1 - 2 * core, tm)
    pair = (wide + (1 - 2 * x_lo) * CORES, tm)

    def send(src, dst, sem, device):
        copy = pltpu.make_async_remote_copy(
            src_ref=src, dst_ref=dst, send_sem=snd.at[sem], recv_sem=rcv.at[sem], device_id=device, device_id_type=MESH
        )
        copy.start()
        return copy

    def drain(ref, sem):
        pltpu.make_async_copy(ref, ref, sem).wait()

    barrier = pltpu.get_barrier_semaphore()

    def greet_xy(d, carry):
        pl.semaphore_signal(barrier, inc=1, device_id=xy_partner(d)[1], device_id_type=MESH)
        return carry

    def greet_z(d, carry):
        pl.semaphore_signal(barrier, inc=1, device_id=z_partner(d)[1], device_id_type=MESH)
        return carry

    lax.fori_loop(1, n_xy, greet_xy, 0)
    lax.fori_loop(1, n_z, greet_z, 0)
    pl.semaphore_signal(barrier, inc=1, device_id=sibling, device_id_type=MESH)

    row_id = lax.broadcasted_iota(jnp.int32, (rows, chan), 0)
    inside = (row_id % LINE) < side
    low_mask = jnp.where(tm > 0, 1.0, 0.0).astype(F32)
    high_mask = jnp.where(tm < n_tm - 1, 1.0, 0.0).astype(F32)
    full = LINE * (side + 2)

    def shifted(ref, f):
        flat = ref[1, f].reshape(full, chan).astype(F32)
        ahead = pltpu.roll(flat, 1, 0).astype(BF16).reshape(side + 2, LINE, chan)
        behind = pltpu.roll(flat, full - 1, 0).astype(BF16).reshape(side + 2, LINE, chan)
        return ahead, behind

    def conv(f):
        xs_ref[1, f] = jnp.zeros((side + 2, LINE, chan), BF16)
        xs_ref[1, f, 1 : side + 1, 0:side, :] = x_ref[0, f]
        ahead, behind = shifted(xs_ref, f)
        xs_ref[0, f] = ahead
        xs_ref[2, f] = behind
        total = jnp.zeros((rows, chan), F32)
        for a in range(3):
            for b in range(3):
                total = total + dot(xs_ref[b, f, a : a + side].reshape(rows, chan), ws_ref[3 * a + b])
        pre_ref[f] = total
        act_ref[f + 1] = jnp.where(inside, total * sigmoid(total), 0.0).astype(BF16)

    left = (wide, (tm + n_tm - 1) % n_tm)
    right = (wide, (tm + 1) % n_tm)

    conv(0)
    conv(frames - 1)
    pl.semaphore_wait(barrier, n_xy - 1 + n_z - 1 + 1)
    to_left = send(act_ref.at[1], act_ref.at[frames + 1], HALO + 1, left)
    to_right = send(act_ref.at[frames], act_ref.at[0], HALO, right)
    for f in range(1, frames - 1):
        conv(f)
    p32 = pr_ref[...].astype(F32)
    pnorm = jnp.sqrt(jnp.sum(p32 * p32, axis=1, keepdims=True) + 1e-06)
    ph_ref[...] = p32 / pnorm

    pooled8 = jnp.zeros((8, chan), F32)
    for f in range(frames):
        pooled8 = pooled8 + jnp.sum(
            xs_ref[1, f, 1 : side + 1].reshape(rows // 8, 8, chan).astype(F32), axis=0
        )
    to_right.wait_recv()
    to_left.wait_recv()
    for f in list(range(1, frames - 1)) + [0, frames - 1]:
        below = dot(act_ref[f], wt_ref[0])
        above = dot(act_ref[f + 2], wt_ref[2])
        if f == 0:
            below = below * low_mask
        if f == frames - 1:
            above = above * high_mask
        pre = below + dot(act_ref[f + 1], wt_ref[1]) + above
        sig = sigmoid(pre)
        pooled8 = pooled8 + jnp.sum((pre * sig).reshape(rows // 8, 8, chan), axis=0)
        dt_ref[f] = jnp.where(inside, sig * (1.0 + pre * (1.0 - sig)), 0.0)
    pool_ref[tm] = pooled8

    def tm_partner(d):
        return (wide, (tm + d) % n_tm)

    def send_pool(d, carry):
        send(pool_ref.at[tm], pool_ref.at[tm], POOL, tm_partner(d))
        return carry

    lax.fori_loop(1, n_tm, send_pool, 0)

    dsend_ref[0] = dt_ref[0].astype(BF16)
    dsend_ref[1] = dt_ref[frames - 1].astype(BF16)
    d_left = send(dsend_ref.at[0], dhalo_ref.at[1], DHALO + 1, left)
    d_right = send(dsend_ref.at[1], dhalo_ref.at[0], DHALO, right)
    for f in range(frames):
        pre_ref[f] = dsilu(pre_ref[f])
        xt_ref[:, f * rows : (f + 1) * rows] = xs_ref[1, f, 1 : side + 1].reshape(rows, chan).T
        actt_ref[:, f * rows : (f + 1) * rows] = act_ref[f + 1].T
        for b in range(3):
            gs_ref[b, f, 0] = jnp.zeros((LINE, chan), BF16)
            gs_ref[b, f, side + 1] = jnp.zeros((LINE, chan), BF16)
    for t in range(3):
        wtt_ref[t] = wt_ref[t].T
    wp = wp_ref[...].astype(F32)
    ids = lax.broadcasted_iota(jnp.int32, (shard, 1), 0) + tm * shard
    multi = jnp.zeros((shard, 1), F32)
    for k in range(pos_ref.shape[1]):
        multi = multi + jnp.where(ids == pos_ref[0, k], 1.0, 0.0)

    drain(pool_ref.at[0 : n_tm - 1], rcv.at[POOL])
    pooled = jnp.sum(jnp.sum(pool_ref[...], axis=0), axis=0, keepdims=True)
    zrow = jnp.sum(wp * to_column(pooled), axis=0, keepdims=True)
    znorm = jnp.sqrt(jnp.sum(zrow * zrow, axis=1, keepdims=True) + 1e-06)
    zhat = zrow / znorm
    expo = jnp.exp(16.0 * jnp.sum(ph_ref[...] * zhat, axis=1, keepdims=True))
    hits = multi * expo
    part_a = jnp.sum(ph_ref[...] * expo, axis=0, keepdims=True)
    part_b = jnp.sum(ph_ref[...] * hits, axis=0, keepdims=True)
    tiles = embed // 128
    for k in range(tiles):
        ab_ref[tm, 0, k : k + 1, :] = part_a[:, 128 * k : 128 * (k + 1)]
        ab_ref[tm, 0, tiles + k : tiles + k + 1, :] = part_b[:, 128 * k : 128 * (k + 1)]
    ab_ref[tm, 1, 0:4, :] = jnp.broadcast_to(jnp.sum(expo, axis=0, keepdims=True), (4, 128))
    ab_ref[tm, 1, 4:8, :] = jnp.broadcast_to(jnp.sum(hits, axis=0, keepdims=True), (4, 128))

    def send_ab(d, carry):
        send(ab_ref.at[tm], ab_ref.at[tm], AB, tm_partner(d))
        return carry

    lax.fori_loop(1, n_tm, send_ab, 0)
    drain(ab_ref.at[0 : n_tm - 1], rcv.at[AB])
    summed = jnp.sum(ab_ref[...], axis=0)
    sum_a = jnp.concatenate([summed[0, k : k + 1] for k in range(tiles)], axis=1)
    sum_b = jnp.concatenate([summed[0, tiles + k : tiles + k + 1] for k in range(tiles)], axis=1)
    total = summed[1, 0:1, 0:1]
    pos_total = summed[1, 4:5, 0:1]
    g_zhat = 16.0 * (sum_a / total - sum_b / pos_total)
    g_z = (g_zhat - zhat * jnp.sum(zhat * g_zhat, axis=1, keepdims=True)) / znorm
    g_pooled = to_row(jnp.sum(wp * g_z, axis=1, keepdims=True))
    g_s = expo / total - hits / pos_total

    for k in range(chan // 128):
        wg_ref[wide, k : k + 1, :] = pooled[:, 128 * k : 128 * (k + 1)]
    for k in range(tiles):
        wg_ref[wide, 2 + k : 3 + k, :] = g_z[:, 128 * k : 128 * (k + 1)]
        wg_ref[wide, 6 + k : 7 + k, :] = zhat[:, 128 * k : 128 * (k + 1)]
        wg_ref[wide, 10 + k : 11 + k, :] = to_row(g_s[128 * k : 128 * (k + 1)])
    wg_ref[wide, 14:16, :] = jnp.zeros((2, 128), F32)
    head_copy = send(wg_ref.at[wide], wg_ref.at[wide], HEAD, sibling)

    for f in range(frames):
        gt_ref[f + 1] = (dt_ref[f] * g_pooled).astype(BF16)
    d_right.wait_recv()
    d_left.wait_recv()
    gt_ref[0] = (dhalo_ref[0].astype(F32) * (g_pooled * low_mask)).astype(BF16)
    gt_ref[frames + 1] = (dhalo_ref[1].astype(F32) * (g_pooled * high_mask)).astype(BF16)

    half = chan // 2
    core_copies = []

    def put(g, t, grad):
        gbuf_ref[g, 0, t] = grad[:half]
        gbuf_ref[g, 1, t] = grad[half:]

    def send_core(g):
        core_copies.append(send(gbuf_ref.at[g, 1 - core], rbuf_ref.at[g], CORE + g, sibling))

    def send_xy(g):
        core_copies[g].wait_recv()
        for t in range(3):
            both = (gbuf_ref[g, core, t] + rbuf_ref[g, t]).astype(BF16)
            for p in range(n_xy):
                i, j = p // 2, p % 2
                cs_ref[g, p, t] = both[16 * i : 16 * (i + 1), 128 * j : 128 * (j + 1)]

        def one(d, carry):
            p, device = xy_partner(d)
            send(cs_ref.at[g, p], xyr_ref.at[g, d - 1], XY + g, device)
            return carry

        lax.fori_loop(1, n_xy, one, 0)

    for t in range(3):
        put(0, t, dot(actt_ref[...], gt_ref[2 - t : 2 - t + frames].reshape(frames * rows, chan)))
    send_core(0)

    for f in range(frames):
        g_act = jnp.zeros((rows, chan), F32)
        for t in range(3):
            g_act = g_act + dot(gt_ref[f + 2 - t], wtt_ref[t])
        gs_ref[1, f, 1 : side + 1] = (g_act * pre_ref[f]).astype(BF16).reshape(side, LINE, chan)
        ahead, behind = shifted(gs_ref, f)
        gs_ref[2, f] = ahead
        gs_ref[0, f] = behind
    send_xy(0)
    head_copy.wait_recv()
    pair_rows = wg_ref.at[pl.ds(wide - core, CORES)]
    pair_copy = send(pair_rows, pair_rows, PAIR, pair)

    for a in range(3):
        for b in range(3):
            window = gs_ref[b, :, 2 - a : 2 - a + side].reshape(frames * rows, chan)
            put(1 + a, b, dot(xt_ref[...], window))
        send_core(1 + a)
        if a == 0:
            pair_copy.wait_recv()
            z_rows = wg_ref.at[pl.ds(z * (CORES * X_LO), CORES * X_LO)]

            def send_head(d, carry):
                send(z_rows, z_rows, ZHEAD, z_partner(d)[1])
                return carry

            lax.fori_loop(1, n_z, send_head, 0)
        if a > 0:
            send_xy(a)
    send_xy(3)

    drain(wg_ref.at[0 : n_wide - CORES * X_LO], rcv.at[ZHEAD])

    def all_clips(first, count):
        return jnp.concatenate([wg_ref[:, first + k, :] for k in range(count)], axis=1)

    over_clips = (((0,), (0,)), ((), ()))
    pooled_all = all_clips(0, chan // 128)
    g_z_all = all_clips(2, tiles)
    zhat_all = all_clips(6, tiles)
    g_s_all = all_clips(10, shard // 128)
    gproj_ref[...] = lax.dot_general(pooled_all, g_z_all, over_clips, precision=HI, preferred_element_type=F32)
    g_phat = 16.0 * lax.dot_general(g_s_all, zhat_all, over_clips, precision=HI, preferred_element_type=F32)
    phat = ph_ref[...]
    p32 = pr_ref[...].astype(F32)
    pnorm = jnp.sqrt(jnp.sum(p32 * p32, axis=1, keepdims=True) + 1e-06)
    gprm_ref[...] = (g_phat - phat * jnp.sum(phat * g_phat, axis=1, keepdims=True)) / pnorm

    for g in range(4):
        drain(xyr_ref.at[g], rcv.at[XY + g])
        value = cs_ref[g, mine].astype(F32)
        for d in range(n_xy - 1):
            value = value + xyr_ref[g, d].astype(F32)
        for t in range(3):
            zsrc_ref[6 * g + 2 * t] = value[t, :8]
            zsrc_ref[6 * g + 2 * t + 1] = value[t, 8:]
    chunk = 24 // n_z

    def send_zsum(d, carry):
        pz, device = z_partner(d)
        send(zsrc_ref.at[pl.ds(pz * chunk, chunk)], zr_ref.at[d - 1], ZSUM, device)
        return carry

    lax.fori_loop(1, n_z, send_zsum, 0)
    drain(zr_ref, rcv.at[ZSUM])
    own = pl.ds(z * chunk, chunk)
    reduced = zsrc_ref[own] + jnp.sum(zr_ref[...], axis=0)
    zred_ref[...] = reduced
    zg_ref[own] = reduced

    def send_zall(d, carry):
        send(zred_ref, zg_ref.at[own], ZALL, z_partner(d)[1])
        return carry

    lax.fori_loop(1, n_z, send_zall, 0)
    drain(zg_ref.at[0 : 24 - chunk], rcv.at[ZALL])
    for q in range(12):
        ag_ref[core, mine, q] = jnp.concatenate([zg_ref[2 * q], zg_ref[2 * q + 1]], axis=0).astype(BF16)
    own_piece = ag_ref.at[core, mine]
    for dx in (0, 1, 3, 2):

        def send_piece(dy, carry):
            send(own_piece, own_piece, XYALL + dx, xy_partner(dx * n_y + dy)[1])
            return carry

        lax.fori_loop(1 if dx == 0 else 0, n_y, send_piece, 0)
    last = []
    for dx in (0, 1, 3, 2):
        count = n_y - 1 if dx == 0 else n_y
        drain(ag_ref.at[0, 0:count], rcv.at[XYALL + dx])
        column = ag_ref.at[core, pl.ds(((x + n_x - dx) % n_x) * n_y, n_y)]
        last.append(send(column, column, COREALL + dx, sibling))
    for copy in last:
        copy.wait_recv()

    for copy in [to_left, to_right, d_left, d_right, head_copy, pair_copy] + core_copies + last:
        copy.wait_send()
    drain(pool_ref.at[0 : n_tm - 1], snd.at[POOL])
    drain(ab_ref.at[0 : n_tm - 1], snd.at[AB])
    drain(wg_ref.at[0 : n_wide - CORES * X_LO], snd.at[ZHEAD])
    for g in range(4):
        drain(xyr_ref.at[g], snd.at[XY + g])
    drain(zr_ref, snd.at[ZSUM])
    drain(zg_ref.at[0 : 24 - chunk], snd.at[ZALL])
    for dx in range(n_x):
        drain(ag_ref.at[0, 0 : n_y - 1 if dx == 0 else n_y], snd.at[XYALL + dx])


def lay_kernel(ag_ref, gproj_ref, gprm_ref, gs_out, gt_out, gproj_out, gprm_out, buf_ref, sems):
    copies = [
        pltpu.make_async_copy(gprm_ref, gprm_out, sems.at[12]),
        pltpu.make_async_copy(gproj_ref, gproj_out, sems.at[13]),
    ]
    for copy in copies:
        copy.start()
    cores, pieces, taps = ag_ref.shape[:3]
    half = buf_ref.shape[1] // cores
    for q in range(taps):
        for c in range(cores):
            for p in range(pieces):
                i, j = p // 2, p % 2
                r = half * c + 16 * i
                buf_ref[q, r : r + 16, 128 * j : 128 * (j + 1)] = ag_ref[c, p, q].astype(F32)
        target = gt_out.at[q] if q < 3 else gs_out.at[q - 3]
        copies.append(pltpu.make_async_copy(buf_ref.at[q], target, sems.at[q]))
        copies[-1].start()
    for copy in copies:
        copy.wait()


def body(clips_in, w_spatial, w_temporal, w_proj, prompts, positives):
    n_wide, n_tm = lax.axis_size("wide"), lax.axis_size("tm")
    clips, frames, side, _, chan = clips_in.shape
    shard, embed = prompts.shape
    rows = side * LINE
    n_z = n_wide // (X_LO * CORES)
    n_xy = X_HI * X_LO * (n_tm // X_HI)
    sizes = (n_wide, n_tm, frames, side, chan, embed, shard)
    vmem = pl.BlockSpec(memory_space=pltpu.VMEM)
    smem = pl.BlockSpec(memory_space=pltpu.SMEM)
    half = chan // 2
    gathered, grad_proj, grad_prompts = pl.pallas_call(
        functools.partial(step_kernel, sizes),
        out_shape=(
            jax.ShapeDtypeStruct((CORES, n_xy, 12, 16, 128), BF16),
            jax.ShapeDtypeStruct((chan, embed), F32),
            jax.ShapeDtypeStruct((shard, embed), F32),
        ),
        in_specs=[vmem] * 5 + [smem],
        out_specs=(vmem, vmem, vmem),
        scratch_shapes=[
            pltpu.VMEM((3, frames, side + 2, LINE, chan), BF16),
            pltpu.VMEM((frames, rows, chan), F32),
            pltpu.VMEM((frames + 2, rows, chan), BF16),
            pltpu.VMEM((frames, rows, chan), F32),
            pltpu.VMEM((2, rows, chan), BF16),
            pltpu.VMEM((2, rows, chan), BF16),
            pltpu.VMEM((frames + 2, rows, chan), BF16),
            pltpu.VMEM((3, frames, side + 2, LINE, chan), BF16),
            pltpu.VMEM((chan, frames * rows), BF16),
            pltpu.VMEM((chan, frames * rows), BF16),
            pltpu.VMEM((3, chan, chan), BF16),
            pltpu.VMEM((shard, embed), F32),
            pltpu.VMEM((n_tm, 8, chan), F32),
            pltpu.VMEM((n_tm, 2, 8, 128), F32),
            pltpu.VMEM((n_wide, 16, 128), F32),
            pltpu.VMEM((4, 2, 3, half, chan), F32),
            pltpu.VMEM((4, 3, half, chan), F32),
            pltpu.VMEM((4, n_xy, 3, 16, 128), BF16),
            pltpu.VMEM((4, n_xy - 1, 3, 16, 128), BF16),
            pltpu.VMEM((24, 8, 128), F32),
            pltpu.VMEM((n_z - 1, 24 // n_z, 8, 128), F32),
            pltpu.VMEM((24 // n_z, 8, 128), F32),
            pltpu.VMEM((24, 8, 128), F32),
            pltpu.SemaphoreType.DMA((SEMS,)),
            pltpu.SemaphoreType.DMA((SEMS,)),
        ],
        compiler_params=pltpu.CompilerParams(
            collective_id=0, has_side_effects=True, vmem_limit_bytes=48 * 1024 * 1024
        ),
        name="step",
    )(clips_in, w_spatial.reshape(9, chan, chan), w_temporal, w_proj, prompts, positives)
    anywhere = pl.BlockSpec(memory_space=pl.ANY)
    grad_s, grad_t, grad_p, grad_m = pl.pallas_call(
        lay_kernel,
        out_shape=(
            jax.ShapeDtypeStruct((9, chan, chan), F32),
            jax.ShapeDtypeStruct((3, chan, chan), F32),
            jax.ShapeDtypeStruct((chan, embed), F32),
            jax.ShapeDtypeStruct((shard, embed), F32),
        ),
        in_specs=[vmem] * 3,
        out_specs=(anywhere,) * 4,
        scratch_shapes=[pltpu.VMEM((12, chan, chan), F32), pltpu.SemaphoreType.DMA((14,))],
        name="lay_out",
    )(gathered, grad_proj, grad_prompts)
    return grad_s.reshape(3, 3, chan, chan), grad_t, grad_p, grad_m


def solution(mesh):
    placed = (P("wide", "tm", None, None, None), P(), P(), P(), P("tm", None), P("wide", None))
    return jax.shard_map(
        body, mesh=mesh, in_specs=placed, out_specs=(P(), P(), P(), P("tm", None)), check_vma=False
    )
```

```python
import functools

import jax
import jax.numpy as jnp
from jax import lax
from jax.experimental import pallas as pl
from jax.experimental.pallas import tpu as pltpu
from jax.sharding import PartitionSpec as P

MESH = pl.DeviceIdType.MESH
F32 = jnp.float32
BF16 = jnp.bfloat16
HI = lax.Precision.HIGHEST

X_LO = 2
X_HI = 2
CORES = 2
LINE = 16

HALO, DHALO, POOL, AB, HEAD, PAIR, ZHEAD, CORE, XY, ZSUM, ZALL, XYALL, COREALL, SEMS = (
    0, 2, 4, 5, 6, 7, 8, 9, 12, 15, 18, 21, 33, 45
)
GROUPS = 3
TAPS = 4


def dot(left, right):
    return jnp.dot(left, right, preferred_element_type=F32)


def sigmoid(v):
    return 1.0 / (1.0 + jnp.exp(-v))


def dsilu(v):
    sig = sigmoid(v)
    return sig * (1.0 + v * (1.0 - sig))


def same(n):
    return lax.broadcasted_iota(jnp.int32, (n, n), 0) == lax.broadcasted_iota(jnp.int32, (n, n), 1)


def to_column(row):
    return jnp.sum(jnp.where(same(row.shape[1]), row, 0.0), axis=1, keepdims=True)


def to_row(column):
    return jnp.sum(jnp.where(same(column.shape[0]), column, 0.0), axis=0, keepdims=True)


def step_kernel(
    sizes,
    x_ref, ws_hbm, wt_hbm, wp_hbm, pr_hbm, pos_hbm,
    ag_ref, gproj_ref, gprm_ref,
    xs_ref, pre_ref, act_ref, dt_ref, dsend_ref, dhalo_ref, gt_ref, gs_ref, xt_ref, actt_ref, wtt_ref,
    ph_ref, pool_ref, ab_ref, wg_ref, gbuf_ref, rbuf_ref, cs_ref, xyr_ref, zsrc_ref, zr_ref, zred_ref, zg_ref,
    ws_ref, wt_ref, wp_ref, pr_ref, pos_ref,
    snd, rcv, loc,
):
    n_wide, n_tm, frames, side, chan, embed, shard = sizes
    rows = side * LINE
    n_z = n_wide // (X_LO * CORES)
    n_y = n_tm // X_HI
    n_x = X_HI * X_LO
    n_xy = n_x * n_y

    wide = lax.axis_index("wide")
    tm = lax.axis_index("tm")
    core = wide % CORES
    x_lo = (wide // CORES) % X_LO
    z = wide // (CORES * X_LO)
    y = tm % n_y
    x = (tm // n_y) * X_LO + x_lo
    mine = x * n_y + y

    def xy_partner(d):
        px = (x + d // n_y) % n_x
        py = (y + d % n_y) % n_y
        return px * n_y + py, (z * (CORES * X_LO) + (px % X_LO) * CORES + core, (px // X_LO) * n_y + py)

    def z_partner(d):
        pz = (z + d) % n_z
        return pz, (pz * (CORES * X_LO) + x_lo * CORES + core, tm)

    sibling = (wide + 1 - 2 * core, tm)
    pair = (wide + (1 - 2 * x_lo) * CORES, tm)

    def send(src, dst, sem, device):
        copy = pltpu.make_async_remote_copy(
            src_ref=src, dst_ref=dst, send_sem=snd.at[sem], recv_sem=rcv.at[sem], device_id=device, device_id_type=MESH
        )
        copy.start()
        return copy

    def drain(ref, sem):
        pltpu.make_async_copy(ref, ref, sem).wait()

    loads = [
        pltpu.make_async_copy(src, dst, loc.at[i])
        for i, (src, dst) in enumerate(
            [(ws_hbm, ws_ref), (pr_hbm, pr_ref), (wt_hbm, wt_ref), (wp_hbm, wp_ref), (pos_hbm, pos_ref)]
        )
    ]
    for load in loads:
        load.start()
    load_ws, load_pr, load_wt, load_wp, load_pos = loads

    barrier = pltpu.get_barrier_semaphore()

    def greet_xy(d, carry):
        pl.semaphore_signal(barrier, inc=1, device_id=xy_partner(d)[1], device_id_type=MESH)
        return carry

    def greet_z(d, carry):
        pl.semaphore_signal(barrier, inc=1, device_id=z_partner(d)[1], device_id_type=MESH)
        return carry

    lax.fori_loop(1, n_xy, greet_xy, 0)
    lax.fori_loop(1, n_z, greet_z, 0)
    pl.semaphore_signal(barrier, inc=1, device_id=sibling, device_id_type=MESH)

    row_id = lax.broadcasted_iota(jnp.int32, (rows, chan), 0)
    inside = (row_id % LINE) < side
    low_mask = jnp.where(tm > 0, 1.0, 0.0).astype(F32)
    high_mask = jnp.where(tm < n_tm - 1, 1.0, 0.0).astype(F32)
    full = LINE * (side + 2)

    def shifted(ref, f):
        flat = ref[1, f].reshape(full, chan).astype(F32)
        ahead = pltpu.roll(flat, 1, 0).astype(BF16).reshape(side + 2, LINE, chan)
        behind = pltpu.roll(flat, full - 1, 0).astype(BF16).reshape(side + 2, LINE, chan)
        return ahead, behind

    def window(f):
        xs_ref[1, f] = jnp.zeros((side + 2, LINE, chan), BF16)
        xs_ref[1, f, 1 : side + 1, 0:side, :] = x_ref[0, f]
        ahead, behind = shifted(xs_ref, f)
        xs_ref[0, f] = ahead
        xs_ref[2, f] = behind

    def conv(f):
        total = jnp.zeros((rows, chan), F32)
        for a in range(3):
            for b in range(3):
                total = total + dot(xs_ref[b, f, a : a + side].reshape(rows, chan), ws_ref[3 * a + b])
        pre_ref[f] = total
        act_ref[f + 1] = jnp.where(inside, total * sigmoid(total), 0.0).astype(BF16)

    left = (wide, (tm + n_tm - 1) % n_tm)
    right = (wide, (tm + 1) % n_tm)

    window(0)
    window(frames - 1)
    load_ws.wait()
    conv(0)
    conv(frames - 1)
    pl.semaphore_wait(barrier, n_xy - 1 + n_z - 1 + 1)
    to_left = send(act_ref.at[1], act_ref.at[frames + 1], HALO + 1, left)
    to_right = send(act_ref.at[frames], act_ref.at[0], HALO, right)
    for f in range(1, frames - 1):
        window(f)
        conv(f)
    load_pr.wait()
    p32 = pr_ref[...].astype(F32)
    pnorm = jnp.sqrt(jnp.sum(p32 * p32, axis=1, keepdims=True) + 1e-06)
    ph_ref[...] = p32 / pnorm

    pooled8 = jnp.zeros((8, chan), F32)
    for f in range(frames):
        pooled8 = pooled8 + jnp.sum(
            xs_ref[1, f, 1 : side + 1].reshape(rows // 8, 8, chan).astype(F32), axis=0
        )
    load_wt.wait()
    to_right.wait_recv()
    to_left.wait_recv()
    for f in list(range(1, frames - 1)) + [0, frames - 1]:
        below = dot(act_ref[f], wt_ref[0])
        above = dot(act_ref[f + 2], wt_ref[2])
        if f == 0:
            below = below * low_mask
        if f == frames - 1:
            above = above * high_mask
        pre = below + dot(act_ref[f + 1], wt_ref[1]) + above
        sig = sigmoid(pre)
        pooled8 = pooled8 + jnp.sum((pre * sig).reshape(rows // 8, 8, chan), axis=0)
        dt_ref[f] = jnp.where(inside, sig * (1.0 + pre * (1.0 - sig)), 0.0)
    pool_ref[tm] = pooled8

    def tm_partner(d):
        return (wide, (tm + d) % n_tm)

    def send_pool(d, carry):
        send(pool_ref.at[tm], pool_ref.at[tm], POOL, tm_partner(d))
        return carry

    lax.fori_loop(1, n_tm, send_pool, 0)

    dsend_ref[0] = dt_ref[0].astype(BF16)
    dsend_ref[1] = dt_ref[frames - 1].astype(BF16)
    d_left = send(dsend_ref.at[0], dhalo_ref.at[1], DHALO + 1, left)
    d_right = send(dsend_ref.at[1], dhalo_ref.at[0], DHALO, right)
    for f in range(frames):
        pre_ref[f] = dsilu(pre_ref[f])
        xt_ref[:, f * rows : (f + 1) * rows] = xs_ref[1, f, 1 : side + 1].reshape(rows, chan).T
        actt_ref[:, f * rows : (f + 1) * rows] = act_ref[f + 1].T
        for b in range(3):
            gs_ref[b, f, 0] = jnp.zeros((LINE, chan), BF16)
            gs_ref[b, f, side + 1] = jnp.zeros((LINE, chan), BF16)
    for t in range(3):
        wtt_ref[t] = wt_ref[t].T
    load_wp.wait()
    load_pos.wait()
    wp = wp_ref[...].astype(F32)
    ids = lax.broadcasted_iota(jnp.int32, (shard, 1), 0) + tm * shard
    multi = jnp.zeros((shard, 1), F32)
    for k in range(pos_ref.shape[1]):
        multi = multi + jnp.where(ids == pos_ref[0:1, k : k + 1], 1.0, 0.0)

    drain(pool_ref.at[0 : n_tm - 1], rcv.at[POOL])
    pooled = jnp.sum(jnp.sum(pool_ref[...], axis=0), axis=0, keepdims=True)
    zrow = jnp.sum(wp * to_column(pooled), axis=0, keepdims=True)
    znorm = jnp.sqrt(jnp.sum(zrow * zrow, axis=1, keepdims=True) + 1e-06)
    zhat = zrow / znorm
    expo = jnp.exp(16.0 * jnp.sum(ph_ref[...] * zhat, axis=1, keepdims=True))
    hits = multi * expo
    part_a = jnp.sum(ph_ref[...] * expo, axis=0, keepdims=True)
    part_b = jnp.sum(ph_ref[...] * hits, axis=0, keepdims=True)
    tiles = embed // 128
    for k in range(tiles):
        ab_ref[tm, 0, k : k + 1, :] = part_a[:, 128 * k : 128 * (k + 1)]
        ab_ref[tm, 0, tiles + k : tiles + k + 1, :] = part_b[:, 128 * k : 128 * (k + 1)]
    ab_ref[tm, 1, 0:4, :] = jnp.broadcast_to(jnp.sum(expo, axis=0, keepdims=True), (4, 128))
    ab_ref[tm, 1, 4:8, :] = jnp.broadcast_to(jnp.sum(hits, axis=0, keepdims=True), (4, 128))

    def send_ab(d, carry):
        send(ab_ref.at[tm], ab_ref.at[tm], AB, tm_partner(d))
        return carry

    lax.fori_loop(1, n_tm, send_ab, 0)
    drain(ab_ref.at[0 : n_tm - 1], rcv.at[AB])
    summed = jnp.sum(ab_ref[...], axis=0)
    sum_a = jnp.concatenate([summed[0, k : k + 1] for k in range(tiles)], axis=1)
    sum_b = jnp.concatenate([summed[0, tiles + k : tiles + k + 1] for k in range(tiles)], axis=1)
    total = summed[1, 0:1, 0:1]
    pos_total = summed[1, 4:5, 0:1]
    g_zhat = 16.0 * (sum_a / total - sum_b / pos_total)
    g_z = (g_zhat - zhat * jnp.sum(zhat * g_zhat, axis=1, keepdims=True)) / znorm
    g_pooled = to_row(jnp.sum(wp * g_z, axis=1, keepdims=True))
    g_s = expo / total - hits / pos_total

    for k in range(chan // 128):
        wg_ref[wide, k : k + 1, :] = pooled[:, 128 * k : 128 * (k + 1)]
    for k in range(tiles):
        wg_ref[wide, 2 + k : 3 + k, :] = g_z[:, 128 * k : 128 * (k + 1)]
        wg_ref[wide, 6 + k : 7 + k, :] = zhat[:, 128 * k : 128 * (k + 1)]
        wg_ref[wide, 10 + k : 11 + k, :] = to_row(g_s[128 * k : 128 * (k + 1)])
    wg_ref[wide, 14:16, :] = jnp.zeros((2, 128), F32)
    head_copy = send(wg_ref.at[wide], wg_ref.at[wide], HEAD, sibling)

    for f in range(frames):
        gt_ref[f + 1] = (dt_ref[f] * g_pooled).astype(BF16)
    d_right.wait_recv()
    d_left.wait_recv()
    gt_ref[0] = (dhalo_ref[0].astype(F32) * (g_pooled * low_mask)).astype(BF16)
    gt_ref[frames + 1] = (dhalo_ref[1].astype(F32) * (g_pooled * high_mask)).astype(BF16)

    half = chan // 2
    core_copies = []

    def put(q, grad):
        g, t = q // TAPS, q % TAPS
        gbuf_ref[g, 0, t] = grad[:half]
        gbuf_ref[g, 1, t] = grad[half:]

    def send_core(g):
        core_copies.append(send(gbuf_ref.at[g, 1 - core], rbuf_ref.at[g], CORE + g, sibling))

    def send_xy(g):
        core_copies[g].wait_recv()
        for t in range(TAPS):
            both = (gbuf_ref[g, core, t] + rbuf_ref[g, t]).astype(BF16)
            for p in range(n_xy):
                i, j = p // 2, p % 2
                cs_ref[g, p, t] = both[16 * i : 16 * (i + 1), 128 * j : 128 * (j + 1)]

        def one(d, carry):
            p, device = xy_partner(d)
            send(cs_ref.at[g, p], xyr_ref.at[g, d - 1], XY + g, device)
            return carry

        lax.fori_loop(1, n_xy, one, 0)

    def put_spatial(q):
        a, b = (q - 3) // 3, (q - 3) % 3
        put(q, dot(xt_ref[...], gs_ref[b, :, 2 - a : 2 - a + side].reshape(frames * rows, chan)))

    def sum_z(g):
        drain(xyr_ref.at[g], rcv.at[XY + g])
        value = cs_ref[g, mine].astype(F32)
        for d in range(n_xy - 1):
            value = value + xyr_ref[g, d].astype(F32)
        for t in range(TAPS):
            zsrc_ref[g, 2 * t] = value[t, :8]
            zsrc_ref[g, 2 * t + 1] = value[t, 8:]

        def one(d, carry):
            pz, device = z_partner(d)
            send(zsrc_ref.at[g, pz], zr_ref.at[g, d - 1], ZSUM + g, device)
            return carry

        lax.fori_loop(1, n_z, one, 0)

    def gather_z(g):
        drain(zr_ref.at[g], rcv.at[ZSUM + g])
        reduced = zsrc_ref[g, z] + jnp.sum(zr_ref[g], axis=0)
        zred_ref[g] = reduced
        zg_ref[g, z] = reduced

        def one(d, carry):
            send(zred_ref.at[g], zg_ref.at[g, z], ZALL + g, z_partner(d)[1])
            return carry

        lax.fori_loop(1, n_z, one, 0)

    def gather_xy(g):
        drain(zg_ref.at[g, 0 : n_z - 1], rcv.at[ZALL + g])
        for t in range(TAPS):
            ag_ref[g, core, mine, t] = jnp.concatenate([zg_ref[g, 2 * t], zg_ref[g, 2 * t + 1]], axis=0).astype(BF16)
        own_piece = ag_ref.at[g, core, mine]
        for dx in (0, 1, 3, 2):

            def one(dy, carry):
                send(own_piece, own_piece, XYALL + n_x * g + dx, xy_partner(dx * n_y + dy)[1])
                return carry

            lax.fori_loop(1 if dx == 0 else 0, n_y, one, 0)

    last = []

    def gather_core(g):
        for dx in (0, 1, 3, 2):
            count = n_y - 1 if dx == 0 else n_y
            drain(ag_ref.at[g, 0, 0:count], rcv.at[XYALL + n_x * g + dx])
            column = ag_ref.at[g, core, pl.ds(((x + n_x - dx) % n_x) * n_y, n_y)]
            last.append(send(column, column, COREALL + n_x * g + dx, sibling))

    for t in range(3):
        put(t, dot(actt_ref[...], gt_ref[2 - t : 2 - t + frames].reshape(frames * rows, chan)))

    for f in range(frames):
        g_act = jnp.zeros((rows, chan), F32)
        for t in range(3):
            g_act = g_act + dot(gt_ref[f + 2 - t], wtt_ref[t])
        gs_ref[1, f, 1 : side + 1] = (g_act * pre_ref[f]).astype(BF16).reshape(side, LINE, chan)
        ahead, behind = shifted(gs_ref, f)
        gs_ref[2, f] = ahead
        gs_ref[0, f] = behind
    put_spatial(3)
    send_core(0)
    head_copy.wait_recv()
    pair_rows = wg_ref.at[pl.ds(wide - core, CORES)]
    pair_copy = send(pair_rows, pair_rows, PAIR, pair)

    for q in range(TAPS, 2 * TAPS):
        put_spatial(q)
    send_core(1)
    send_xy(0)
    pair_copy.wait_recv()
    z_rows = wg_ref.at[pl.ds(z * (CORES * X_LO), CORES * X_LO)]

    def send_head(d, carry):
        send(z_rows, z_rows, ZHEAD, z_partner(d)[1])
        return carry

    lax.fori_loop(1, n_z, send_head, 0)
    for q in range(2 * TAPS, 3 * TAPS):
        put_spatial(q)
    send_core(2)
    send_xy(1)
    send_xy(2)
    sum_z(0)

    drain(wg_ref.at[0 : n_wide - CORES * X_LO], rcv.at[ZHEAD])

    def all_clips(first, count):
        return jnp.concatenate([wg_ref[:, first + k, :] for k in range(count)], axis=1)

    over_clips = (((0,), (0,)), ((), ()))
    pooled_all = all_clips(0, chan // 128)
    g_z_all = all_clips(2, tiles)
    zhat_all = all_clips(6, tiles)
    g_s_all = all_clips(10, shard // 128)
    gproj_ref[...] = lax.dot_general(pooled_all, g_z_all, over_clips, precision=HI, preferred_element_type=F32)
    sum_z(1)
    g_phat = 16.0 * lax.dot_general(g_s_all, zhat_all, over_clips, precision=HI, preferred_element_type=F32)
    phat = ph_ref[...]
    p32 = pr_ref[...].astype(F32)
    pnorm = jnp.sqrt(jnp.sum(p32 * p32, axis=1, keepdims=True) + 1e-06)
    gprm_ref[...] = (g_phat - phat * jnp.sum(phat * g_phat, axis=1, keepdims=True)) / pnorm

    gather_z(0)
    sum_z(2)
    gather_z(1)
    gather_xy(0)
    gather_z(2)
    gather_xy(1)
    gather_core(0)
    gather_xy(2)
    gather_core(1)
    gather_core(2)
    for copy in last:
        copy.wait_recv()

    for copy in [to_left, to_right, d_left, d_right, head_copy, pair_copy] + core_copies + last:
        copy.wait_send()
    drain(pool_ref.at[0 : n_tm - 1], snd.at[POOL])
    drain(ab_ref.at[0 : n_tm - 1], snd.at[AB])
    drain(wg_ref.at[0 : n_wide - CORES * X_LO], snd.at[ZHEAD])
    for g in range(GROUPS):
        drain(xyr_ref.at[g], snd.at[XY + g])
        drain(zr_ref.at[g], snd.at[ZSUM + g])
        drain(zg_ref.at[g, 0 : n_z - 1], snd.at[ZALL + g])
        for dx in range(n_x):
            drain(ag_ref.at[g, 0, 0 : n_y - 1 if dx == 0 else n_y], snd.at[XYALL + n_x * g + dx])


def lay_kernel(ag_ref, gproj_ref, gprm_ref, gs_out, gt_out, gproj_out, gprm_out, buf_ref, sems):
    copies = [
        pltpu.make_async_copy(gprm_ref, gprm_out, sems.at[12]),
        pltpu.make_async_copy(gproj_ref, gproj_out, sems.at[13]),
    ]
    for copy in copies:
        copy.start()
    groups, cores, pieces, taps = ag_ref.shape[:4]
    half = buf_ref.shape[1] // cores
    for q in range(groups * taps):
        for c in range(cores):
            for p in range(pieces):
                i, j = p // 2, p % 2
                r = half * c + 16 * i
                buf_ref[q, r : r + 16, 128 * j : 128 * (j + 1)] = ag_ref[q // taps, c, p, q % taps].astype(F32)
        target = gt_out.at[q] if q < 3 else gs_out.at[q - 3]
        copies.append(pltpu.make_async_copy(buf_ref.at[q], target, sems.at[q]))
        copies[-1].start()
    for copy in copies:
        copy.wait()


def body(clips_in, w_spatial, w_temporal, w_proj, prompts, positives):
    n_wide, n_tm = lax.axis_size("wide"), lax.axis_size("tm")
    clips, frames, side, _, chan = clips_in.shape
    shard, embed = prompts.shape
    rows = side * LINE
    n_z = n_wide // (X_LO * CORES)
    n_xy = X_HI * X_LO * (n_tm // X_HI)
    sizes = (n_wide, n_tm, frames, side, chan, embed, shard)
    vmem = pl.BlockSpec(memory_space=pltpu.VMEM)
    hbm = pl.BlockSpec(memory_space=pltpu.HBM)
    half = chan // 2
    gathered, grad_proj, grad_prompts = pl.pallas_call(
        functools.partial(step_kernel, sizes),
        out_shape=(
            jax.ShapeDtypeStruct((GROUPS, CORES, n_xy, TAPS, 16, 128), BF16),
            jax.ShapeDtypeStruct((chan, embed), F32),
            jax.ShapeDtypeStruct((shard, embed), F32),
        ),
        in_specs=[vmem] + [hbm] * 5,
        out_specs=(vmem, vmem, vmem),
        scratch_shapes=[
            pltpu.VMEM((3, frames, side + 2, LINE, chan), BF16),
            pltpu.VMEM((frames, rows, chan), F32),
            pltpu.VMEM((frames + 2, rows, chan), BF16),
            pltpu.VMEM((frames, rows, chan), F32),
            pltpu.VMEM((2, rows, chan), BF16),
            pltpu.VMEM((2, rows, chan), BF16),
            pltpu.VMEM((frames + 2, rows, chan), BF16),
            pltpu.VMEM((3, frames, side + 2, LINE, chan), BF16),
            pltpu.VMEM((chan, frames * rows), BF16),
            pltpu.VMEM((chan, frames * rows), BF16),
            pltpu.VMEM((3, chan, chan), BF16),
            pltpu.VMEM((shard, embed), F32),
            pltpu.VMEM((n_tm, 8, chan), F32),
            pltpu.VMEM((n_tm, 2, 8, 128), F32),
            pltpu.VMEM((n_wide, 16, 128), F32),
            pltpu.VMEM((GROUPS, 2, TAPS, half, chan), F32),
            pltpu.VMEM((GROUPS, TAPS, half, chan), F32),
            pltpu.VMEM((GROUPS, n_xy, TAPS, 16, 128), BF16),
            pltpu.VMEM((GROUPS, n_xy - 1, TAPS, 16, 128), BF16),
            pltpu.VMEM((GROUPS, n_z, 8, 128), F32),
            pltpu.VMEM((GROUPS, n_z - 1, 8, 128), F32),
            pltpu.VMEM((GROUPS, 8, 128), F32),
            pltpu.VMEM((GROUPS, n_z, 8, 128), F32),
            pltpu.VMEM((9, chan, chan), BF16),
            pltpu.VMEM((3, chan, chan), BF16),
            pltpu.VMEM((chan, embed), BF16),
            pltpu.VMEM((shard, embed), BF16),
            pltpu.VMEM(positives.shape, jnp.int32),
            pltpu.SemaphoreType.DMA((SEMS,)),
            pltpu.SemaphoreType.DMA((SEMS,)),
            pltpu.SemaphoreType.DMA((5,)),
        ],
        compiler_params=pltpu.CompilerParams(
            collective_id=0, has_side_effects=True, vmem_limit_bytes=48 * 1024 * 1024
        ),
        name="step",
    )(clips_in, w_spatial.reshape(9, chan, chan), w_temporal, w_proj, prompts, positives)
    anywhere = pl.BlockSpec(memory_space=pl.ANY)
    grad_s, grad_t, grad_p, grad_m = pl.pallas_call(
        lay_kernel,
        out_shape=(
            jax.ShapeDtypeStruct((9, chan, chan), F32),
            jax.ShapeDtypeStruct((3, chan, chan), F32),
            jax.ShapeDtypeStruct((chan, embed), F32),
            jax.ShapeDtypeStruct((shard, embed), F32),
        ),
        in_specs=[vmem] * 3,
        out_specs=(anywhere,) * 4,
        scratch_shapes=[pltpu.VMEM((12, chan, chan), F32), pltpu.SemaphoreType.DMA((14,))],
        compiler_params=pltpu.CompilerParams(vmem_limit_bytes=8 * 1024 * 1024),
        name="lay_out",
    )(gathered, grad_proj, grad_prompts)
    return grad_s.reshape(3, 3, chan, chan), grad_t, grad_p, grad_m


def solution(mesh):
    placed = (P("wide", "tm", None, None, None), P(), P(), P(), P("tm", None), P("wide", None))
    return jax.shard_map(
        body, mesh=mesh, in_specs=placed, out_specs=(P(), P(), P(), P("tm", None)), check_vma=False
    )
```

```python
import functools

import jax
import jax.numpy as jnp
from jax import lax
from jax.experimental import pallas as pl
from jax.experimental.pallas import tpu as pltpu
from jax.sharding import PartitionSpec as P

MESH = pl.DeviceIdType.MESH
F32 = jnp.float32
BF16 = jnp.bfloat16
HI = lax.Precision.HIGHEST

X_LO = 2
X_HI = 2
CORES = 2
LINE = 16

HALO, DHALO, POOL, AB, HEAD, PAIR, ZHEAD, CORE, XY, ZSUM, ZALL, XYALL, COREALL, SEMS = (
    0, 2, 4, 5, 6, 7, 8, 9, 12, 15, 18, 21, 33, 45
)
GROUPS = 3
TAPS = 4


def dot(left, right):
    return jnp.dot(left, right, preferred_element_type=F32)


def sigmoid(v):
    return 1.0 / (1.0 + jnp.exp(-v))


def dsilu(v):
    sig = sigmoid(v)
    return sig * (1.0 + v * (1.0 - sig))


def same(n):
    return lax.broadcasted_iota(jnp.int32, (n, n), 0) == lax.broadcasted_iota(jnp.int32, (n, n), 1)


def to_column(row):
    return jnp.sum(jnp.where(same(row.shape[1]), row, 0.0), axis=1, keepdims=True)


def to_row(column):
    return jnp.sum(jnp.where(same(column.shape[0]), column, 0.0), axis=0, keepdims=True)


def step_kernel(
    sizes,
    x_hbm, ws_hbm, wt_hbm, wp_hbm, pr_hbm, pos_hbm,
    ag_hbm, gproj_hbm, gprm_hbm,
    xs_ref, pre_ref, act_ref, dt_ref, dsend_ref, dhalo_ref, gt_ref, gs_ref, xt_ref, actt_ref, wtt_ref,
    ph_ref, pool_ref, ab_ref, wg_ref, gbuf_ref, rbuf_ref, cs_ref, xyr_ref, zsrc_ref, zr_ref, zred_ref, zg_ref,
    ws_ref, wt_ref, wp_ref, pr_ref, pos_ref, x_ref, ag_ref, gproj_ref, gprm_ref,
    snd, rcv, loc, out,
):
    n_wide, n_tm, frames, side, chan, embed, shard = sizes
    rows = side * LINE
    n_z = n_wide // (X_LO * CORES)
    n_y = n_tm // X_HI
    n_x = X_HI * X_LO
    n_xy = n_x * n_y

    wide = lax.axis_index("wide")
    tm = lax.axis_index("tm")
    core = wide % CORES
    x_lo = (wide // CORES) % X_LO
    z = wide // (CORES * X_LO)
    y = tm % n_y
    x = (tm // n_y) * X_LO + x_lo
    mine = x * n_y + y

    def xy_partner(d):
        px = (x + d // n_y) % n_x
        py = (y + d % n_y) % n_y
        return px * n_y + py, (z * (CORES * X_LO) + (px % X_LO) * CORES + core, (px // X_LO) * n_y + py)

    def z_partner(d):
        pz = (z + d) % n_z
        return pz, (pz * (CORES * X_LO) + x_lo * CORES + core, tm)

    sibling = (wide + 1 - 2 * core, tm)
    pair = (wide + (1 - 2 * x_lo) * CORES, tm)

    def send(src, dst, sem, device):
        copy = pltpu.make_async_remote_copy(
            src_ref=src, dst_ref=dst, send_sem=snd.at[sem], recv_sem=rcv.at[sem], device_id=device, device_id_type=MESH
        )
        copy.start()
        return copy

    def drain(ref, sem):
        pltpu.make_async_copy(ref, ref, sem).wait()

    loads = [
        pltpu.make_async_copy(src, dst, loc.at[i])
        for i, (src, dst) in enumerate(
            [
                (x_hbm, x_ref), (ws_hbm, ws_ref), (pr_hbm, pr_ref),
                (wt_hbm, wt_ref), (wp_hbm, wp_ref), (pos_hbm, pos_ref),
            ]
        )
    ]
    for load in loads:
        load.start()
    load_x, load_ws, load_pr, load_wt, load_wp, load_pos = loads

    barrier = pltpu.get_barrier_semaphore()

    def greet_xy(d, carry):
        pl.semaphore_signal(barrier, inc=1, device_id=xy_partner(d)[1], device_id_type=MESH)
        return carry

    def greet_z(d, carry):
        pl.semaphore_signal(barrier, inc=1, device_id=z_partner(d)[1], device_id_type=MESH)
        return carry

    lax.fori_loop(1, n_xy, greet_xy, 0)
    lax.fori_loop(1, n_z, greet_z, 0)
    pl.semaphore_signal(barrier, inc=1, device_id=sibling, device_id_type=MESH)

    row_id = lax.broadcasted_iota(jnp.int32, (rows, chan), 0)
    inside = (row_id % LINE) < side
    low_mask = jnp.where(tm > 0, 1.0, 0.0).astype(F32)
    high_mask = jnp.where(tm < n_tm - 1, 1.0, 0.0).astype(F32)
    full = LINE * (side + 2)

    def shifted(ref, f):
        flat = ref[1, f].reshape(full, chan).astype(F32)
        ahead = pltpu.roll(flat, 1, 0).astype(BF16).reshape(side + 2, LINE, chan)
        behind = pltpu.roll(flat, full - 1, 0).astype(BF16).reshape(side + 2, LINE, chan)
        return ahead, behind

    def window(f):
        xs_ref[1, f] = jnp.zeros((side + 2, LINE, chan), BF16)
        xs_ref[1, f, 1 : side + 1, 0:side, :] = x_ref[0, f]
        ahead, behind = shifted(xs_ref, f)
        xs_ref[0, f] = ahead
        xs_ref[2, f] = behind

    def conv(f):
        total = jnp.zeros((rows, chan), F32)
        for a in range(3):
            for b in range(3):
                total = total + dot(xs_ref[b, f, a : a + side].reshape(rows, chan), ws_ref[3 * a + b])
        pre_ref[f] = total
        act_ref[f + 1] = jnp.where(inside, total * sigmoid(total), 0.0).astype(BF16)

    left = (wide, (tm + n_tm - 1) % n_tm)
    right = (wide, (tm + 1) % n_tm)

    load_x.wait()
    window(0)
    window(frames - 1)
    load_ws.wait()
    conv(0)
    conv(frames - 1)
    pl.semaphore_wait(barrier, n_xy - 1 + n_z - 1 + 1)
    to_left = send(act_ref.at[1], act_ref.at[frames + 1], HALO + 1, left)
    to_right = send(act_ref.at[frames], act_ref.at[0], HALO, right)
    for f in range(1, frames - 1):
        window(f)
        conv(f)
    load_pr.wait()
    p32 = pr_ref[...].astype(F32)
    pnorm = jnp.sqrt(jnp.sum(p32 * p32, axis=1, keepdims=True) + 1e-06)
    ph_ref[...] = p32 / pnorm

    pooled8 = jnp.zeros((8, chan), F32)
    for f in range(frames):
        pooled8 = pooled8 + jnp.sum(
            xs_ref[1, f, 1 : side + 1].reshape(rows // 8, 8, chan).astype(F32), axis=0
        )
    load_wt.wait()
    to_right.wait_recv()
    to_left.wait_recv()
    for f in list(range(1, frames - 1)) + [0, frames - 1]:
        below = dot(act_ref[f], wt_ref[0])
        above = dot(act_ref[f + 2], wt_ref[2])
        if f == 0:
            below = below * low_mask
        if f == frames - 1:
            above = above * high_mask
        pre = below + dot(act_ref[f + 1], wt_ref[1]) + above
        sig = sigmoid(pre)
        pooled8 = pooled8 + jnp.sum((pre * sig).reshape(rows // 8, 8, chan), axis=0)
        dt_ref[f] = jnp.where(inside, sig * (1.0 + pre * (1.0 - sig)), 0.0)
    pool_ref[tm] = pooled8

    def tm_partner(d):
        return (wide, (tm + d) % n_tm)

    def send_pool(d, carry):
        send(pool_ref.at[tm], pool_ref.at[tm], POOL, tm_partner(d))
        return carry

    lax.fori_loop(1, n_tm, send_pool, 0)

    dsend_ref[0] = dt_ref[0].astype(BF16)
    dsend_ref[1] = dt_ref[frames - 1].astype(BF16)
    d_left = send(dsend_ref.at[0], dhalo_ref.at[1], DHALO + 1, left)
    d_right = send(dsend_ref.at[1], dhalo_ref.at[0], DHALO, right)
    for f in range(frames):
        pre_ref[f] = dsilu(pre_ref[f])
        xt_ref[:, f * rows : (f + 1) * rows] = xs_ref[1, f, 1 : side + 1].reshape(rows, chan).T
        actt_ref[:, f * rows : (f + 1) * rows] = act_ref[f + 1].T
        for b in range(3):
            gs_ref[b, f, 0] = jnp.zeros((LINE, chan), BF16)
            gs_ref[b, f, side + 1] = jnp.zeros((LINE, chan), BF16)
    for t in range(3):
        wtt_ref[t] = wt_ref[t].T
    load_wp.wait()
    load_pos.wait()
    wp = wp_ref[...].astype(F32)
    ids = lax.broadcasted_iota(jnp.int32, (shard, 1), 0) + tm * shard
    multi = jnp.zeros((shard, 1), F32)
    for k in range(pos_ref.shape[1]):
        multi = multi + jnp.where(ids == pos_ref[0:1, k : k + 1], 1.0, 0.0)

    drain(pool_ref.at[0 : n_tm - 1], rcv.at[POOL])
    pooled = jnp.sum(jnp.sum(pool_ref[...], axis=0), axis=0, keepdims=True)
    zrow = jnp.sum(wp * to_column(pooled), axis=0, keepdims=True)
    znorm = jnp.sqrt(jnp.sum(zrow * zrow, axis=1, keepdims=True) + 1e-06)
    zhat = zrow / znorm
    expo = jnp.exp(16.0 * jnp.sum(ph_ref[...] * zhat, axis=1, keepdims=True))
    hits = multi * expo
    part_a = jnp.sum(ph_ref[...] * expo, axis=0, keepdims=True)
    part_b = jnp.sum(ph_ref[...] * hits, axis=0, keepdims=True)
    tiles = embed // 128
    for k in range(tiles):
        ab_ref[tm, 0, k : k + 1, :] = part_a[:, 128 * k : 128 * (k + 1)]
        ab_ref[tm, 0, tiles + k : tiles + k + 1, :] = part_b[:, 128 * k : 128 * (k + 1)]
    ab_ref[tm, 1, 0:4, :] = jnp.broadcast_to(jnp.sum(expo, axis=0, keepdims=True), (4, 128))
    ab_ref[tm, 1, 4:8, :] = jnp.broadcast_to(jnp.sum(hits, axis=0, keepdims=True), (4, 128))

    def send_ab(d, carry):
        send(ab_ref.at[tm], ab_ref.at[tm], AB, tm_partner(d))
        return carry

    lax.fori_loop(1, n_tm, send_ab, 0)
    drain(ab_ref.at[0 : n_tm - 1], rcv.at[AB])
    summed = jnp.sum(ab_ref[...], axis=0)
    sum_a = jnp.concatenate([summed[0, k : k + 1] for k in range(tiles)], axis=1)
    sum_b = jnp.concatenate([summed[0, tiles + k : tiles + k + 1] for k in range(tiles)], axis=1)
    total = summed[1, 0:1, 0:1]
    pos_total = summed[1, 4:5, 0:1]
    g_zhat = 16.0 * (sum_a / total - sum_b / pos_total)
    g_z = (g_zhat - zhat * jnp.sum(zhat * g_zhat, axis=1, keepdims=True)) / znorm
    g_pooled = to_row(jnp.sum(wp * g_z, axis=1, keepdims=True))
    g_s = expo / total - hits / pos_total

    for k in range(chan // 128):
        wg_ref[wide, k : k + 1, :] = pooled[:, 128 * k : 128 * (k + 1)]
    for k in range(tiles):
        wg_ref[wide, 2 + k : 3 + k, :] = g_z[:, 128 * k : 128 * (k + 1)]
        wg_ref[wide, 6 + k : 7 + k, :] = zhat[:, 128 * k : 128 * (k + 1)]
        wg_ref[wide, 10 + k : 11 + k, :] = to_row(g_s[128 * k : 128 * (k + 1)])
    wg_ref[wide, 14:16, :] = jnp.zeros((2, 128), F32)
    head_copy = send(wg_ref.at[wide], wg_ref.at[wide], HEAD, sibling)

    for f in range(frames):
        gt_ref[f + 1] = (dt_ref[f] * g_pooled).astype(BF16)
    d_right.wait_recv()
    d_left.wait_recv()
    gt_ref[0] = (dhalo_ref[0].astype(F32) * (g_pooled * low_mask)).astype(BF16)
    gt_ref[frames + 1] = (dhalo_ref[1].astype(F32) * (g_pooled * high_mask)).astype(BF16)

    half = chan // 2
    core_copies = []

    def put(q, grad):
        g, t = q // TAPS, q % TAPS
        gbuf_ref[g, 0, t] = grad[:half]
        gbuf_ref[g, 1, t] = grad[half:]

    def send_core(g):
        core_copies.append(send(gbuf_ref.at[g, 1 - core], rbuf_ref.at[g], CORE + g, sibling))

    def send_xy(g):
        core_copies[g].wait_recv()
        for t in range(TAPS):
            both = (gbuf_ref[g, core, t] + rbuf_ref[g, t]).astype(BF16)
            for p in range(n_xy):
                i, j = p // 2, p % 2
                cs_ref[g, p, t] = both[16 * i : 16 * (i + 1), 128 * j : 128 * (j + 1)]

        def one(d, carry):
            p, device = xy_partner(d)
            send(cs_ref.at[g, p], xyr_ref.at[g, d - 1], XY + g, device)
            return carry

        lax.fori_loop(1, n_xy, one, 0)

    def put_spatial(q):
        a, b = (q - 3) // 3, (q - 3) % 3
        put(q, dot(xt_ref[...], gs_ref[b, :, 2 - a : 2 - a + side].reshape(frames * rows, chan)))

    def sum_z(g):
        drain(xyr_ref.at[g], rcv.at[XY + g])
        value = cs_ref[g, mine].astype(F32)
        for d in range(n_xy - 1):
            value = value + xyr_ref[g, d].astype(F32)
        for t in range(TAPS):
            zsrc_ref[g, 2 * t] = value[t, :8]
            zsrc_ref[g, 2 * t + 1] = value[t, 8:]

        def one(d, carry):
            pz, device = z_partner(d)
            send(zsrc_ref.at[g, pz], zr_ref.at[g, d - 1], ZSUM + g, device)
            return carry

        lax.fori_loop(1, n_z, one, 0)

    def gather_z(g):
        drain(zr_ref.at[g], rcv.at[ZSUM + g])
        reduced = zsrc_ref[g, z] + jnp.sum(zr_ref[g], axis=0)
        zred_ref[g] = reduced
        zg_ref[g, z] = reduced

        def one(d, carry):
            send(zred_ref.at[g], zg_ref.at[g, z], ZALL + g, z_partner(d)[1])
            return carry

        lax.fori_loop(1, n_z, one, 0)

    def gather_xy(g):
        drain(zg_ref.at[g, 0 : n_z - 1], rcv.at[ZALL + g])
        for t in range(TAPS):
            ag_ref[g, core, mine, t] = jnp.concatenate([zg_ref[g, 2 * t], zg_ref[g, 2 * t + 1]], axis=0).astype(BF16)
        own_piece = ag_ref.at[g, core, mine]
        for dx in (0, 1, 3, 2):

            def one(dy, carry):
                send(own_piece, own_piece, XYALL + n_x * g + dx, xy_partner(dx * n_y + dy)[1])
                return carry

            lax.fori_loop(1 if dx == 0 else 0, n_y, one, 0)

    last = []

    def gather_core(g):
        for dx in (0, 1, 3, 2):
            count = n_y - 1 if dx == 0 else n_y
            drain(ag_ref.at[g, 0, 0:count], rcv.at[XYALL + n_x * g + dx])
            column = ag_ref.at[g, core, pl.ds(((x + n_x - dx) % n_x) * n_y, n_y)]
            last.append(send(column, column, COREALL + n_x * g + dx, sibling))

    for t in range(3):
        put(t, dot(actt_ref[...], gt_ref[2 - t : 2 - t + frames].reshape(frames * rows, chan)))

    for f in range(frames):
        g_act = jnp.zeros((rows, chan), F32)
        for t in range(3):
            g_act = g_act + dot(gt_ref[f + 2 - t], wtt_ref[t])
        gs_ref[1, f, 1 : side + 1] = (g_act * pre_ref[f]).astype(BF16).reshape(side, LINE, chan)
        ahead, behind = shifted(gs_ref, f)
        gs_ref[2, f] = ahead
        gs_ref[0, f] = behind
    put_spatial(3)
    send_core(0)
    head_copy.wait_recv()
    pair_rows = wg_ref.at[pl.ds(wide - core, CORES)]
    pair_copy = send(pair_rows, pair_rows, PAIR, pair)

    for q in range(TAPS, 2 * TAPS):
        put_spatial(q)
    send_core(1)
    send_xy(0)
    pair_copy.wait_recv()
    z_rows = wg_ref.at[pl.ds(z * (CORES * X_LO), CORES * X_LO)]

    def send_head(d, carry):
        send(z_rows, z_rows, ZHEAD, z_partner(d)[1])
        return carry

    lax.fori_loop(1, n_z, send_head, 0)
    for q in range(2 * TAPS, 3 * TAPS):
        put_spatial(q)
    send_core(2)
    send_xy(1)
    send_xy(2)
    sum_z(0)

    drain(wg_ref.at[0 : n_wide - CORES * X_LO], rcv.at[ZHEAD])

    def all_clips(first, count):
        return jnp.concatenate([wg_ref[:, first + k, :] for k in range(count)], axis=1)

    over_clips = (((0,), (0,)), ((), ()))
    pooled_all = all_clips(0, chan // 128)
    g_z_all = all_clips(2, tiles)
    zhat_all = all_clips(6, tiles)
    g_s_all = all_clips(10, shard // 128)
    gproj_ref[...] = lax.dot_general(pooled_all, g_z_all, over_clips, precision=HI, preferred_element_type=F32)
    sum_z(1)
    g_phat = 16.0 * lax.dot_general(g_s_all, zhat_all, over_clips, precision=HI, preferred_element_type=F32)
    phat = ph_ref[...]
    p32 = pr_ref[...].astype(F32)
    pnorm = jnp.sqrt(jnp.sum(p32 * p32, axis=1, keepdims=True) + 1e-06)
    gprm_ref[...] = (g_phat - phat * jnp.sum(phat * g_phat, axis=1, keepdims=True)) / pnorm
    results = [
        pltpu.make_async_copy(gproj_ref, gproj_hbm, out.at[GROUPS]),
        pltpu.make_async_copy(gprm_ref, gprm_hbm, out.at[GROUPS + 1]),
    ]
    for result in results:
        result.start()

    def put_out(g):
        for copy in last[n_x * g : n_x * (g + 1)]:
            copy.wait_recv()
        result = pltpu.make_async_copy(ag_ref.at[g], ag_hbm.at[g], out.at[g])
        result.start()
        results.append(result)

    gather_z(0)
    sum_z(2)
    gather_z(1)
    gather_xy(0)
    gather_z(2)
    gather_xy(1)
    gather_core(0)
    gather_xy(2)
    gather_core(1)
    put_out(0)
    gather_core(2)
    put_out(1)
    put_out(2)

    for copy in [to_left, to_right, d_left, d_right, head_copy, pair_copy] + core_copies + last:
        copy.wait_send()
    drain(pool_ref.at[0 : n_tm - 1], snd.at[POOL])
    drain(ab_ref.at[0 : n_tm - 1], snd.at[AB])
    drain(wg_ref.at[0 : n_wide - CORES * X_LO], snd.at[ZHEAD])
    for g in range(GROUPS):
        drain(xyr_ref.at[g], snd.at[XY + g])
        drain(zr_ref.at[g], snd.at[ZSUM + g])
        drain(zg_ref.at[g, 0 : n_z - 1], snd.at[ZALL + g])
        for dx in range(n_x):
            drain(ag_ref.at[g, 0, 0 : n_y - 1 if dx == 0 else n_y], snd.at[XYALL + n_x * g + dx])
    for result in results:
        result.wait()


def lay_kernel(
    ag_hbm, gproj_hbm, gprm_hbm, gs_out, gt_out, gproj_out, gprm_out,
    ag_ref, gproj_ref, gprm_ref, buf_ref, load_sems, sems,
):
    groups, cores, pieces, taps = ag_ref.shape[:4]
    loads = [pltpu.make_async_copy(ag_hbm.at[g], ag_ref.at[g], load_sems.at[g]) for g in range(groups)]
    loads.append(pltpu.make_async_copy(gprm_hbm, gprm_ref, load_sems.at[groups]))
    loads.append(pltpu.make_async_copy(gproj_hbm, gproj_ref, load_sems.at[groups + 1]))
    for load in loads:
        load.start()
    copies = []
    half = buf_ref.shape[1] // cores
    for q in range(groups * taps):
        if q % taps == 0:
            loads[q // taps].wait()
        for c in range(cores):
            for p in range(pieces):
                i, j = p // 2, p % 2
                r = half * c + 16 * i
                buf_ref[q, r : r + 16, 128 * j : 128 * (j + 1)] = ag_ref[q // taps, c, p, q % taps].astype(F32)
        target = gt_out.at[q] if q < 3 else gs_out.at[q - 3]
        copies.append(pltpu.make_async_copy(buf_ref.at[q], target, sems.at[q]))
        copies[-1].start()
    loads[groups].wait()
    copies.append(pltpu.make_async_copy(gprm_ref, gprm_out, sems.at[12]))
    copies[-1].start()
    loads[groups + 1].wait()
    copies.append(pltpu.make_async_copy(gproj_ref, gproj_out, sems.at[13]))
    copies[-1].start()
    for copy in copies:
        copy.wait()


def body(clips_in, w_spatial, w_temporal, w_proj, prompts, positives):
    n_wide, n_tm = lax.axis_size("wide"), lax.axis_size("tm")
    clips, frames, side, _, chan = clips_in.shape
    shard, embed = prompts.shape
    rows = side * LINE
    n_z = n_wide // (X_LO * CORES)
    n_xy = X_HI * X_LO * (n_tm // X_HI)
    sizes = (n_wide, n_tm, frames, side, chan, embed, shard)
    hbm = pl.BlockSpec(memory_space=pltpu.HBM)
    half = chan // 2
    gathered, grad_proj, grad_prompts = pl.pallas_call(
        functools.partial(step_kernel, sizes),
        out_shape=(
            jax.ShapeDtypeStruct((GROUPS, CORES, n_xy, TAPS, 16, 128), BF16),
            jax.ShapeDtypeStruct((chan, embed), F32),
            jax.ShapeDtypeStruct((shard, embed), F32),
        ),
        in_specs=[hbm] * 6,
        out_specs=(hbm,) * 3,
        scratch_shapes=[
            pltpu.VMEM((3, frames, side + 2, LINE, chan), BF16),
            pltpu.VMEM((frames, rows, chan), F32),
            pltpu.VMEM((frames + 2, rows, chan), BF16),
            pltpu.VMEM((frames, rows, chan), F32),
            pltpu.VMEM((2, rows, chan), BF16),
            pltpu.VMEM((2, rows, chan), BF16),
            pltpu.VMEM((frames + 2, rows, chan), BF16),
            pltpu.VMEM((3, frames, side + 2, LINE, chan), BF16),
            pltpu.VMEM((chan, frames * rows), BF16),
            pltpu.VMEM((chan, frames * rows), BF16),
            pltpu.VMEM((3, chan, chan), BF16),
            pltpu.VMEM((shard, embed), F32),
            pltpu.VMEM((n_tm, 8, chan), F32),
            pltpu.VMEM((n_tm, 2, 8, 128), F32),
            pltpu.VMEM((n_wide, 16, 128), F32),
            pltpu.VMEM((GROUPS, 2, TAPS, half, chan), F32),
            pltpu.VMEM((GROUPS, TAPS, half, chan), F32),
            pltpu.VMEM((GROUPS, n_xy, TAPS, 16, 128), BF16),
            pltpu.VMEM((GROUPS, n_xy - 1, TAPS, 16, 128), BF16),
            pltpu.VMEM((GROUPS, n_z, 8, 128), F32),
            pltpu.VMEM((GROUPS, n_z - 1, 8, 128), F32),
            pltpu.VMEM((GROUPS, 8, 128), F32),
            pltpu.VMEM((GROUPS, n_z, 8, 128), F32),
            pltpu.VMEM((9, chan, chan), BF16),
            pltpu.VMEM((3, chan, chan), BF16),
            pltpu.VMEM((chan, embed), BF16),
            pltpu.VMEM((shard, embed), BF16),
            pltpu.VMEM(positives.shape, jnp.int32),
            pltpu.VMEM(clips_in.shape, BF16),
            pltpu.VMEM((GROUPS, CORES, n_xy, TAPS, 16, 128), BF16),
            pltpu.VMEM((chan, embed), F32),
            pltpu.VMEM((shard, embed), F32),
            pltpu.SemaphoreType.DMA((SEMS,)),
            pltpu.SemaphoreType.DMA((SEMS,)),
            pltpu.SemaphoreType.DMA((6,)),
            pltpu.SemaphoreType.DMA((GROUPS + 2,)),
        ],
        compiler_params=pltpu.CompilerParams(
            collective_id=0, has_side_effects=True, vmem_limit_bytes=66_500_000
        ),
        name="step",
    )(clips_in, w_spatial.reshape(9, chan, chan), w_temporal, w_proj, prompts, positives)
    grad_s, grad_t, grad_p, grad_m = pl.pallas_call(
        lay_kernel,
        out_shape=(
            jax.ShapeDtypeStruct((9, chan, chan), F32),
            jax.ShapeDtypeStruct((3, chan, chan), F32),
            jax.ShapeDtypeStruct((chan, embed), F32),
            jax.ShapeDtypeStruct((shard, embed), F32),
        ),
        in_specs=[hbm] * 3,
        out_specs=(hbm,) * 4,
        scratch_shapes=[
            pltpu.VMEM((GROUPS, CORES, n_xy, TAPS, 16, 128), BF16),
            pltpu.VMEM((chan, embed), F32),
            pltpu.VMEM((shard, embed), F32),
            pltpu.VMEM((12, chan, chan), F32),
            pltpu.SemaphoreType.DMA((GROUPS + 2,)),
            pltpu.SemaphoreType.DMA((14,)),
        ],
        compiler_params=pltpu.CompilerParams(vmem_limit_bytes=66_500_000),
        name="lay_out",
    )(gathered, grad_proj, grad_prompts)
    return grad_s.reshape(3, 3, chan, chan), grad_t, grad_p, grad_m


def solution(mesh):
    placed = (P("wide", "tm", None, None, None), P(), P(), P(), P("tm", None), P("wide", None))
    return jax.shard_map(
        body, mesh=mesh, in_specs=placed, out_specs=(P(), P(), P(), P("tm", None)), check_vma=False
    )
```

```python
import functools

import jax
import jax.numpy as jnp
from jax import lax
from jax.experimental import pallas as pl
from jax.experimental.pallas import tpu as pltpu
from jax.sharding import PartitionSpec as P

MESH = pl.DeviceIdType.MESH
F32 = jnp.float32
BF16 = jnp.bfloat16
HI = lax.Precision.HIGHEST

X_LO = 2
X_HI = 2
CORES = 2
LINE = 16

HALO, DHALO, POOL, AB, HEAD, PAIR, ZHEAD, CORE, XY, ZSUM, ZALL, XYALL, COREALL, SEMS = (
    0, 2, 4, 5, 6, 7, 8, 9, 12, 15, 18, 21, 33, 45
)
GROUPS = 3
TAPS = 4


def dot(left, right):
    return jnp.dot(left, right, preferred_element_type=F32)


def sigmoid(v):
    return 1.0 / (1.0 + jnp.exp(-v))


def dsilu(v):
    sig = sigmoid(v)
    return sig * (1.0 + v * (1.0 - sig))


def same(n):
    return lax.broadcasted_iota(jnp.int32, (n, n), 0) == lax.broadcasted_iota(jnp.int32, (n, n), 1)


def to_column(row):
    return jnp.sum(jnp.where(same(row.shape[1]), row, 0.0), axis=1, keepdims=True)


def to_row(column):
    return jnp.sum(jnp.where(same(column.shape[0]), column, 0.0), axis=0, keepdims=True)


def step_kernel(
    sizes,
    x_hbm, ws_hbm, wt_hbm, wp_hbm, pr_hbm, pos_hbm,
    ag_hbm, gproj_hbm, gprm_hbm,
    xs_ref, pre_ref, act_ref, dt_ref, dsend_ref, dhalo_ref, gt_ref, gs_ref, xt_ref, actt_ref, wtt_ref,
    ph_ref, pool_ref, ab_ref, wg_ref, gbuf_ref, rbuf_ref, cs_ref, xyr_ref, zsrc_ref, zr_ref, zred_ref, zg_ref,
    ws_ref, wt_ref, wp_ref, pr_ref, pos_ref, x_ref, ag_ref, gproj_ref, gprm_ref,
    snd, rcv, loc, out,
):
    n_wide, n_tm, frames, side, chan, embed, shard = sizes
    rows = side * LINE
    n_z = n_wide // (X_LO * CORES)
    n_y = n_tm // X_HI
    n_x = X_HI * X_LO
    n_xy = n_x * n_y

    wide = lax.axis_index("wide")
    tm = lax.axis_index("tm")
    core = wide % CORES
    x_lo = (wide // CORES) % X_LO
    z = wide // (CORES * X_LO)
    y = tm % n_y
    x = (tm // n_y) * X_LO + x_lo
    mine = x * n_y + y

    def xy_partner(d):
        px = (x + d // n_y) % n_x
        py = (y + d % n_y) % n_y
        return px * n_y + py, (z * (CORES * X_LO) + (px % X_LO) * CORES + core, (px // X_LO) * n_y + py)

    def z_partner(d):
        pz = (z + d) % n_z
        return pz, (pz * (CORES * X_LO) + x_lo * CORES + core, tm)

    sibling = (wide + 1 - 2 * core, tm)
    pair = (wide + (1 - 2 * x_lo) * CORES, tm)

    def send(src, dst, sem, device):
        copy = pltpu.make_async_remote_copy(
            src_ref=src, dst_ref=dst, send_sem=snd.at[sem], recv_sem=rcv.at[sem], device_id=device, device_id_type=MESH
        )
        copy.start()
        return copy

    def drain(ref, sem):
        pltpu.make_async_copy(ref, ref, sem).wait()

    loads = [
        pltpu.make_async_copy(src, dst, loc.at[i])
        for i, (src, dst) in enumerate(
            [
                (x_hbm, x_ref), (ws_hbm, ws_ref), (pr_hbm, pr_ref),
                (wt_hbm, wt_ref), (wp_hbm, wp_ref), (pos_hbm, pos_ref),
            ]
        )
    ]
    for load in loads:
        load.start()
    load_x, load_ws, load_pr, load_wt, load_wp, load_pos = loads

    barrier = pltpu.get_barrier_semaphore()

    def greet_xy(d, carry):
        pl.semaphore_signal(barrier, inc=1, device_id=xy_partner(d)[1], device_id_type=MESH)
        return carry

    def greet_z(d, carry):
        pl.semaphore_signal(barrier, inc=1, device_id=z_partner(d)[1], device_id_type=MESH)
        return carry

    lax.fori_loop(1, n_xy, greet_xy, 0)
    lax.fori_loop(1, n_z, greet_z, 0)
    pl.semaphore_signal(barrier, inc=1, device_id=sibling, device_id_type=MESH)

    row_id = lax.broadcasted_iota(jnp.int32, (rows, chan), 0)
    inside = (row_id % LINE) < side
    low_mask = jnp.where(tm > 0, 1.0, 0.0).astype(F32)
    high_mask = jnp.where(tm < n_tm - 1, 1.0, 0.0).astype(F32)
    full = LINE * (side + 2)

    def shifted(ref, f):
        flat = ref[1, f].reshape(full, chan).astype(F32)
        ahead = pltpu.roll(flat, 1, 0).astype(BF16).reshape(side + 2, LINE, chan)
        behind = pltpu.roll(flat, full - 1, 0).astype(BF16).reshape(side + 2, LINE, chan)
        return ahead, behind

    def window(f):
        xs_ref[1, f] = jnp.zeros((side + 2, LINE, chan), BF16)
        xs_ref[1, f, 1 : side + 1, 0:side, :] = x_ref[0, f]
        ahead, behind = shifted(xs_ref, f)
        xs_ref[0, f] = ahead
        xs_ref[2, f] = behind

    def conv(f):
        total = jnp.zeros((rows, chan), F32)
        for a in range(3):
            for b in range(3):
                total = total + dot(xs_ref[b, f, a : a + side].reshape(rows, chan), ws_ref[3 * a + b])
        pre_ref[f] = total
        act_ref[f + 1] = jnp.where(inside, total * sigmoid(total), 0.0).astype(BF16)

    left = (wide, (tm + n_tm - 1) % n_tm)
    right = (wide, (tm + 1) % n_tm)

    load_x.wait()
    window(0)
    window(frames - 1)
    load_ws.wait()
    conv(0)
    conv(frames - 1)
    pl.semaphore_wait(barrier, n_xy - 1 + n_z - 1 + 1)
    to_left = send(act_ref.at[1], act_ref.at[frames + 1], HALO + 1, left)
    to_right = send(act_ref.at[frames], act_ref.at[0], HALO, right)
    for f in range(1, frames - 1):
        window(f)
        conv(f)

    pooled8 = jnp.zeros((8, chan), F32)
    for f in range(frames):
        pooled8 = pooled8 + jnp.sum(
            xs_ref[1, f, 1 : side + 1].reshape(rows // 8, 8, chan).astype(F32), axis=0
        )
    load_wt.wait()
    for f in list(range(1, frames - 1)) + [0, frames - 1]:
        if f == 0:
            to_right.wait_recv()
        if f == frames - 1:
            to_left.wait_recv()
        below = dot(act_ref[f], wt_ref[0])
        above = dot(act_ref[f + 2], wt_ref[2])
        if f == 0:
            below = below * low_mask
        if f == frames - 1:
            above = above * high_mask
        pre = below + dot(act_ref[f + 1], wt_ref[1]) + above
        sig = sigmoid(pre)
        pooled8 = pooled8 + jnp.sum((pre * sig).reshape(rows // 8, 8, chan), axis=0)
        dt_ref[f] = jnp.where(inside, sig * (1.0 + pre * (1.0 - sig)), 0.0)
    pool_ref[tm] = pooled8

    def tm_partner(d):
        return (wide, (tm + d) % n_tm)

    def send_pool(d, carry):
        send(pool_ref.at[tm], pool_ref.at[tm], POOL, tm_partner(d))
        return carry

    lax.fori_loop(1, n_tm, send_pool, 0)

    dsend_ref[0] = dt_ref[0].astype(BF16)
    dsend_ref[1] = dt_ref[frames - 1].astype(BF16)
    d_left = send(dsend_ref.at[0], dhalo_ref.at[1], DHALO + 1, left)
    d_right = send(dsend_ref.at[1], dhalo_ref.at[0], DHALO, right)
    for f in range(frames):
        actt_ref[:, f * rows : (f + 1) * rows] = act_ref[f + 1].T
        for b in range(3):
            gs_ref[b, f, 0] = jnp.zeros((LINE, chan), BF16)
            gs_ref[b, f, side + 1] = jnp.zeros((LINE, chan), BF16)
    for t in range(3):
        wtt_ref[t] = wt_ref[t].T
    load_pr.wait()
    p32 = pr_ref[...].astype(F32)
    pnorm = jnp.sqrt(jnp.sum(p32 * p32, axis=1, keepdims=True) + 1e-06)
    ph_ref[...] = p32 / pnorm
    load_wp.wait()
    load_pos.wait()
    wp = wp_ref[...].astype(F32)
    ids = lax.broadcasted_iota(jnp.int32, (shard, 1), 0) + tm * shard
    multi = jnp.zeros((shard, 1), F32)
    for k in range(pos_ref.shape[1]):
        multi = multi + jnp.where(ids == pos_ref[0:1, k : k + 1], 1.0, 0.0)

    drain(pool_ref.at[0 : n_tm - 1], rcv.at[POOL])
    pooled = jnp.sum(jnp.sum(pool_ref[...], axis=0), axis=0, keepdims=True)
    zrow = jnp.sum(wp * to_column(pooled), axis=0, keepdims=True)
    znorm = jnp.sqrt(jnp.sum(zrow * zrow, axis=1, keepdims=True) + 1e-06)
    zhat = zrow / znorm
    expo = jnp.exp(16.0 * jnp.sum(ph_ref[...] * zhat, axis=1, keepdims=True))
    hits = multi * expo
    part_a = jnp.sum(ph_ref[...] * expo, axis=0, keepdims=True)
    part_b = jnp.sum(ph_ref[...] * hits, axis=0, keepdims=True)
    tiles = embed // 128
    for k in range(tiles):
        ab_ref[tm, 0, k : k + 1, :] = part_a[:, 128 * k : 128 * (k + 1)]
        ab_ref[tm, 0, tiles + k : tiles + k + 1, :] = part_b[:, 128 * k : 128 * (k + 1)]
    ab_ref[tm, 1, 0:4, :] = jnp.broadcast_to(jnp.sum(expo, axis=0, keepdims=True), (4, 128))
    ab_ref[tm, 1, 4:8, :] = jnp.broadcast_to(jnp.sum(hits, axis=0, keepdims=True), (4, 128))

    def send_ab(d, carry):
        send(ab_ref.at[tm], ab_ref.at[tm], AB, tm_partner(d))
        return carry

    lax.fori_loop(1, n_tm, send_ab, 0)
    for f in range(frames):
        pre_ref[f] = dsilu(pre_ref[f])
        xt_ref[:, f * rows : (f + 1) * rows] = xs_ref[1, f, 1 : side + 1].reshape(rows, chan).T
    drain(ab_ref.at[0 : n_tm - 1], rcv.at[AB])
    summed = jnp.sum(ab_ref[...], axis=0)
    sum_a = jnp.concatenate([summed[0, k : k + 1] for k in range(tiles)], axis=1)
    sum_b = jnp.concatenate([summed[0, tiles + k : tiles + k + 1] for k in range(tiles)], axis=1)
    total = summed[1, 0:1, 0:1]
    pos_total = summed[1, 4:5, 0:1]
    g_zhat = 16.0 * (sum_a / total - sum_b / pos_total)
    g_z = (g_zhat - zhat * jnp.sum(zhat * g_zhat, axis=1, keepdims=True)) / znorm
    g_pooled = to_row(jnp.sum(wp * g_z, axis=1, keepdims=True))
    g_s = expo / total - hits / pos_total

    for k in range(chan // 128):
        wg_ref[wide, k : k + 1, :] = pooled[:, 128 * k : 128 * (k + 1)]
    for k in range(tiles):
        wg_ref[wide, 2 + k : 3 + k, :] = g_z[:, 128 * k : 128 * (k + 1)]
        wg_ref[wide, 6 + k : 7 + k, :] = zhat[:, 128 * k : 128 * (k + 1)]
        wg_ref[wide, 10 + k : 11 + k, :] = to_row(g_s[128 * k : 128 * (k + 1)])
    wg_ref[wide, 14:16, :] = jnp.zeros((2, 128), F32)
    head_copy = send(wg_ref.at[wide], wg_ref.at[wide], HEAD, sibling)

    for f in range(frames):
        gt_ref[f + 1] = (dt_ref[f] * g_pooled).astype(BF16)
    d_right.wait_recv()
    d_left.wait_recv()
    gt_ref[0] = (dhalo_ref[0].astype(F32) * (g_pooled * low_mask)).astype(BF16)
    gt_ref[frames + 1] = (dhalo_ref[1].astype(F32) * (g_pooled * high_mask)).astype(BF16)

    half = chan // 2
    core_copies = []

    def put(q, grad):
        g, t = q // TAPS, q % TAPS
        gbuf_ref[g, 0, t] = grad[:half]
        gbuf_ref[g, 1, t] = grad[half:]

    def send_core(g):
        core_copies.append(send(gbuf_ref.at[g, 1 - core], rbuf_ref.at[g], CORE + g, sibling))

    def send_xy(g):
        core_copies[g].wait_recv()
        for t in range(TAPS):
            both = (gbuf_ref[g, core, t] + rbuf_ref[g, t]).astype(BF16)
            for p in range(n_xy):
                i, j = p // 2, p % 2
                cs_ref[g, p, t] = both[16 * i : 16 * (i + 1), 128 * j : 128 * (j + 1)]

        def one(d, carry):
            p, device = xy_partner(d)
            send(cs_ref.at[g, p], xyr_ref.at[g, d - 1], XY + g, device)
            return carry

        lax.fori_loop(1, n_xy, one, 0)

    def put_spatial(q):
        a, b = (q - 3) // 3, (q - 3) % 3
        put(q, dot(xt_ref[...], gs_ref[b, :, 2 - a : 2 - a + side].reshape(frames * rows, chan)))

    def sum_z(g):
        drain(xyr_ref.at[g], rcv.at[XY + g])
        value = cs_ref[g, mine].astype(F32)
        for d in range(n_xy - 1):
            value = value + xyr_ref[g, d].astype(F32)
        for t in range(TAPS):
            zsrc_ref[g, 2 * t] = value[t, :8]
            zsrc_ref[g, 2 * t + 1] = value[t, 8:]

        def one(d, carry):
            pz, device = z_partner(d)
            send(zsrc_ref.at[g, pz], zr_ref.at[g, d - 1], ZSUM + g, device)
            return carry

        lax.fori_loop(1, n_z, one, 0)

    def gather_z(g):
        drain(zr_ref.at[g], rcv.at[ZSUM + g])
        reduced = zsrc_ref[g, z] + jnp.sum(zr_ref[g], axis=0)
        zred_ref[g] = reduced
        zg_ref[g, z] = reduced

        def one(d, carry):
            send(zred_ref.at[g], zg_ref.at[g, z], ZALL + g, z_partner(d)[1])
            return carry

        lax.fori_loop(1, n_z, one, 0)

    def gather_xy(g):
        drain(zg_ref.at[g, 0 : n_z - 1], rcv.at[ZALL + g])
        for t in range(TAPS):
            ag_ref[g, core, mine, t] = jnp.concatenate([zg_ref[g, 2 * t], zg_ref[g, 2 * t + 1]], axis=0).astype(BF16)
        own_piece = ag_ref.at[g, core, mine]
        for dx in (0, 1, 3, 2):

            def one(dy, carry):
                send(own_piece, own_piece, XYALL + n_x * g + dx, xy_partner(dx * n_y + dy)[1])
                return carry

            lax.fori_loop(1 if dx == 0 else 0, n_y, one, 0)

    last = []

    def gather_core(g):
        for dx in (0, 1, 3, 2):
            count = n_y - 1 if dx == 0 else n_y
            drain(ag_ref.at[g, 0, 0:count], rcv.at[XYALL + n_x * g + dx])
            column = ag_ref.at[g, core, pl.ds(((x + n_x - dx) % n_x) * n_y, n_y)]
            last.append(send(column, column, COREALL + n_x * g + dx, sibling))

    for t in range(3):
        put(t, dot(actt_ref[...], gt_ref[2 - t : 2 - t + frames].reshape(frames * rows, chan)))

    for f in range(frames):
        g_act = jnp.zeros((rows, chan), F32)
        for t in range(3):
            g_act = g_act + dot(gt_ref[f + 2 - t], wtt_ref[t])
        gs_ref[1, f, 1 : side + 1] = (g_act * pre_ref[f]).astype(BF16).reshape(side, LINE, chan)
        ahead, behind = shifted(gs_ref, f)
        gs_ref[2, f] = ahead
        gs_ref[0, f] = behind
    put_spatial(3)
    send_core(0)
    head_copy.wait_recv()
    pair_rows = wg_ref.at[pl.ds(wide - core, CORES)]
    pair_copy = send(pair_rows, pair_rows, PAIR, pair)

    for q in range(TAPS, 2 * TAPS):
        put_spatial(q)
    send_core(1)
    send_xy(0)
    pair_copy.wait_recv()
    z_rows = wg_ref.at[pl.ds(z * (CORES * X_LO), CORES * X_LO)]

    def send_head(d, carry):
        send(z_rows, z_rows, ZHEAD, z_partner(d)[1])
        return carry

    lax.fori_loop(1, n_z, send_head, 0)
    for q in range(2 * TAPS, 3 * TAPS):
        put_spatial(q)
    send_core(2)
    send_xy(1)
    send_xy(2)
    sum_z(0)

    drain(wg_ref.at[0 : n_wide - CORES * X_LO], rcv.at[ZHEAD])

    def all_clips(first, count):
        return jnp.concatenate([wg_ref[:, first + k, :] for k in range(count)], axis=1)

    over_clips = (((0,), (0,)), ((), ()))
    pooled_all = all_clips(0, chan // 128)
    g_z_all = all_clips(2, tiles)
    zhat_all = all_clips(6, tiles)
    g_s_all = all_clips(10, shard // 128)
    gproj_ref[...] = lax.dot_general(pooled_all, g_z_all, over_clips, precision=HI, preferred_element_type=F32)
    sum_z(1)
    g_phat = 16.0 * lax.dot_general(g_s_all, zhat_all, over_clips, precision=HI, preferred_element_type=F32)
    phat = ph_ref[...]
    p32 = pr_ref[...].astype(F32)
    pnorm = jnp.sqrt(jnp.sum(p32 * p32, axis=1, keepdims=True) + 1e-06)
    gprm_ref[...] = (g_phat - phat * jnp.sum(phat * g_phat, axis=1, keepdims=True)) / pnorm
    results = [
        pltpu.make_async_copy(gproj_ref, gproj_hbm, out.at[GROUPS]),
        pltpu.make_async_copy(gprm_ref, gprm_hbm, out.at[GROUPS + 1]),
    ]
    for result in results:
        result.start()

    def put_out(g):
        for copy in last[n_x * g : n_x * (g + 1)]:
            copy.wait_recv()
        result = pltpu.make_async_copy(ag_ref.at[g], ag_hbm.at[g], out.at[g])
        result.start()
        results.append(result)

    gather_z(0)
    sum_z(2)
    gather_z(1)
    gather_xy(0)
    gather_z(2)
    gather_xy(1)
    gather_core(0)
    gather_xy(2)
    gather_core(1)
    put_out(0)
    gather_core(2)
    put_out(1)
    put_out(2)

    for copy in [to_left, to_right, d_left, d_right, head_copy, pair_copy] + core_copies + last:
        copy.wait_send()
    drain(pool_ref.at[0 : n_tm - 1], snd.at[POOL])
    drain(ab_ref.at[0 : n_tm - 1], snd.at[AB])
    drain(wg_ref.at[0 : n_wide - CORES * X_LO], snd.at[ZHEAD])
    for g in range(GROUPS):
        drain(xyr_ref.at[g], snd.at[XY + g])
        drain(zr_ref.at[g], snd.at[ZSUM + g])
        drain(zg_ref.at[g, 0 : n_z - 1], snd.at[ZALL + g])
        for dx in range(n_x):
            drain(ag_ref.at[g, 0, 0 : n_y - 1 if dx == 0 else n_y], snd.at[XYALL + n_x * g + dx])
    for result in results:
        result.wait()


def lay_kernel(
    ag_hbm, gproj_hbm, gprm_hbm, gs_out, gt_out, gproj_out, gprm_out,
    ag_ref, gproj_ref, gprm_ref, buf_ref, load_sems, sems,
):
    groups, cores, pieces, taps = ag_ref.shape[:4]
    loads = [pltpu.make_async_copy(ag_hbm.at[g], ag_ref.at[g], load_sems.at[g]) for g in range(groups)]
    loads.append(pltpu.make_async_copy(gprm_hbm, gprm_ref, load_sems.at[groups]))
    loads.append(pltpu.make_async_copy(gproj_hbm, gproj_ref, load_sems.at[groups + 1]))
    for load in loads:
        load.start()
    copies = []
    half = buf_ref.shape[1] // cores
    for q in range(groups * taps):
        if q % taps == 0:
            loads[q // taps].wait()
        for c in range(cores):
            for p in range(pieces):
                i, j = p // 2, p % 2
                r = half * c + 16 * i
                buf_ref[q, r : r + 16, 128 * j : 128 * (j + 1)] = ag_ref[q // taps, c, p, q % taps].astype(F32)
        target = gt_out.at[q] if q < 3 else gs_out.at[q - 3]
        copies.append(pltpu.make_async_copy(buf_ref.at[q], target, sems.at[q]))
        copies[-1].start()
    loads[groups].wait()
    copies.append(pltpu.make_async_copy(gprm_ref, gprm_out, sems.at[12]))
    copies[-1].start()
    loads[groups + 1].wait()
    copies.append(pltpu.make_async_copy(gproj_ref, gproj_out, sems.at[13]))
    copies[-1].start()
    for copy in copies:
        copy.wait()


def body(clips_in, w_spatial, w_temporal, w_proj, prompts, positives):
    n_wide, n_tm = lax.axis_size("wide"), lax.axis_size("tm")
    clips, frames, side, _, chan = clips_in.shape
    shard, embed = prompts.shape
    rows = side * LINE
    n_z = n_wide // (X_LO * CORES)
    n_xy = X_HI * X_LO * (n_tm // X_HI)
    sizes = (n_wide, n_tm, frames, side, chan, embed, shard)
    hbm = pl.BlockSpec(memory_space=pltpu.HBM)
    half = chan // 2
    gathered, grad_proj, grad_prompts = pl.pallas_call(
        functools.partial(step_kernel, sizes),
        out_shape=(
            jax.ShapeDtypeStruct((GROUPS, CORES, n_xy, TAPS, 16, 128), BF16),
            jax.ShapeDtypeStruct((chan, embed), F32),
            jax.ShapeDtypeStruct((shard, embed), F32),
        ),
        in_specs=[hbm] * 6,
        out_specs=(hbm,) * 3,
        scratch_shapes=[
            pltpu.VMEM((3, frames, side + 2, LINE, chan), BF16),
            pltpu.VMEM((frames, rows, chan), F32),
            pltpu.VMEM((frames + 2, rows, chan), BF16),
            pltpu.VMEM((frames, rows, chan), F32),
            pltpu.VMEM((2, rows, chan), BF16),
            pltpu.VMEM((2, rows, chan), BF16),
            pltpu.VMEM((frames + 2, rows, chan), BF16),
            pltpu.VMEM((3, frames, side + 2, LINE, chan), BF16),
            pltpu.VMEM((chan, frames * rows), BF16),
            pltpu.VMEM((chan, frames * rows), BF16),
            pltpu.VMEM((3, chan, chan), BF16),
            pltpu.VMEM((shard, embed), F32),
            pltpu.VMEM((n_tm, 8, chan), F32),
            pltpu.VMEM((n_tm, 2, 8, 128), F32),
            pltpu.VMEM((n_wide, 16, 128), F32),
            pltpu.VMEM((GROUPS, 2, TAPS, half, chan), F32),
            pltpu.VMEM((GROUPS, TAPS, half, chan), F32),
            pltpu.VMEM((GROUPS, n_xy, TAPS, 16, 128), BF16),
            pltpu.VMEM((GROUPS, n_xy - 1, TAPS, 16, 128), BF16),
            pltpu.VMEM((GROUPS, n_z, 8, 128), F32),
            pltpu.VMEM((GROUPS, n_z - 1, 8, 128), F32),
            pltpu.VMEM((GROUPS, 8, 128), F32),
            pltpu.VMEM((GROUPS, n_z, 8, 128), F32),
            pltpu.VMEM((9, chan, chan), BF16),
            pltpu.VMEM((3, chan, chan), BF16),
            pltpu.VMEM((chan, embed), BF16),
            pltpu.VMEM((shard, embed), BF16),
            pltpu.VMEM(positives.shape, jnp.int32),
            pltpu.VMEM(clips_in.shape, BF16),
            pltpu.VMEM((GROUPS, CORES, n_xy, TAPS, 16, 128), BF16),
            pltpu.VMEM((chan, embed), F32),
            pltpu.VMEM((shard, embed), F32),
            pltpu.SemaphoreType.DMA((SEMS,)),
            pltpu.SemaphoreType.DMA((SEMS,)),
            pltpu.SemaphoreType.DMA((6,)),
            pltpu.SemaphoreType.DMA((GROUPS + 2,)),
        ],
        compiler_params=pltpu.CompilerParams(
            collective_id=0, has_side_effects=True, vmem_limit_bytes=66_500_000
        ),
        name="step",
    )(clips_in, w_spatial.reshape(9, chan, chan), w_temporal, w_proj, prompts, positives)
    grad_s, grad_t, grad_p, grad_m = pl.pallas_call(
        lay_kernel,
        out_shape=(
            jax.ShapeDtypeStruct((9, chan, chan), F32),
            jax.ShapeDtypeStruct((3, chan, chan), F32),
            jax.ShapeDtypeStruct((chan, embed), F32),
            jax.ShapeDtypeStruct((shard, embed), F32),
        ),
        in_specs=[hbm] * 3,
        out_specs=(hbm,) * 4,
        scratch_shapes=[
            pltpu.VMEM((GROUPS, CORES, n_xy, TAPS, 16, 128), BF16),
            pltpu.VMEM((chan, embed), F32),
            pltpu.VMEM((shard, embed), F32),
            pltpu.VMEM((12, chan, chan), F32),
            pltpu.SemaphoreType.DMA((GROUPS + 2,)),
            pltpu.SemaphoreType.DMA((14,)),
        ],
        compiler_params=pltpu.CompilerParams(vmem_limit_bytes=66_500_000),
        name="lay_out",
    )(gathered, grad_proj, grad_prompts)
    return grad_s.reshape(3, 3, chan, chan), grad_t, grad_p, grad_m


def solution(mesh):
    placed = (P("wide", "tm", None, None, None), P(), P(), P(), P("tm", None), P("wide", None))
    return jax.shard_map(
        body, mesh=mesh, in_specs=placed, out_specs=(P(), P(), P(), P("tm", None)), check_vma=False
    )
```

```python
import functools

import jax
import jax.numpy as jnp
from jax import lax
from jax.experimental import pallas as pl
from jax.experimental.pallas import tpu as pltpu
from jax.sharding import PartitionSpec as P

MESH = pl.DeviceIdType.MESH
F32 = jnp.float32
BF16 = jnp.bfloat16
HI = lax.Precision.HIGHEST

X_LO = 2
X_HI = 2
CORES = 2
LINE = 16

HALO, DHALO, POOL, AB, HEAD, PAIR, ZHEAD, CORE, XY, ZSUM, ZALL, XYALL, COREALL, SEMS = (
    0, 2, 4, 5, 6, 7, 8, 9, 12, 15, 18, 21, 33, 45
)
GROUPS = 3
TAPS = 4


def dot(left, right):
    return jnp.dot(left, right, preferred_element_type=F32)


def sigmoid(v):
    return 1.0 / (1.0 + jnp.exp(-v))


def dsilu(v):
    sig = sigmoid(v)
    return sig * (1.0 + v * (1.0 - sig))


def same(n):
    return lax.broadcasted_iota(jnp.int32, (n, n), 0) == lax.broadcasted_iota(jnp.int32, (n, n), 1)


def to_column(row):
    return jnp.sum(jnp.where(same(row.shape[1]), row, 0.0), axis=1, keepdims=True)


def to_row(column):
    return jnp.sum(jnp.where(same(column.shape[0]), column, 0.0), axis=0, keepdims=True)


def step_kernel(
    sizes,
    x_hbm, ws_hbm, wt_hbm, wp_hbm, pr_hbm, pos_hbm,
    ag_hbm, gproj_hbm, gprm_hbm,
    xs_ref, pre_ref, act_ref, dt_ref, dsend_ref, dhalo_ref, gt_ref, gs_ref, xt_ref, actt_ref, wtt_ref,
    ph_ref, pool_ref, ab_ref, wg_ref, gbuf_ref, rbuf_ref, cs_ref, xyr_ref, zsrc_ref, zr_ref, zred_ref, zg_ref,
    ws_ref, wt_ref, wp_ref, pr_ref, pos_ref, x_ref, ag_ref, gproj_ref, gprm_ref,
    snd, rcv, loc, out,
):
    n_wide, n_tm, frames, side, chan, embed, shard = sizes
    rows = side * LINE
    n_z = n_wide // (X_LO * CORES)
    n_y = n_tm // X_HI
    n_x = X_HI * X_LO
    n_xy = n_x * n_y

    wide = lax.axis_index("wide")
    tm = lax.axis_index("tm")
    core = wide % CORES
    x_lo = (wide // CORES) % X_LO
    z = wide // (CORES * X_LO)
    y = tm % n_y
    x = (tm // n_y) * X_LO + x_lo
    mine = x * n_y + y

    def xy_partner(d):
        px = (x + d // n_y) % n_x
        py = (y + d % n_y) % n_y
        return px * n_y + py, (z * (CORES * X_LO) + (px % X_LO) * CORES + core, (px // X_LO) * n_y + py)

    def z_partner(d):
        pz = (z + d) % n_z
        return pz, (pz * (CORES * X_LO) + x_lo * CORES + core, tm)

    sibling = (wide + 1 - 2 * core, tm)
    pair = (wide + (1 - 2 * x_lo) * CORES, tm)

    def send(src, dst, sem, device):
        copy = pltpu.make_async_remote_copy(
            src_ref=src, dst_ref=dst, send_sem=snd.at[sem], recv_sem=rcv.at[sem], device_id=device, device_id_type=MESH
        )
        copy.start()
        return copy

    def drain(ref, sem):
        pltpu.make_async_copy(ref, ref, sem).wait()

    loads = [
        pltpu.make_async_copy(src, dst, loc.at[i])
        for i, (src, dst) in enumerate(
            [
                (x_hbm, x_ref), (ws_hbm, ws_ref), (pr_hbm, pr_ref),
                (wt_hbm, wt_ref), (wp_hbm, wp_ref), (pos_hbm, pos_ref),
            ]
        )
    ]
    for load in loads:
        load.start()
    load_x, load_ws, load_pr, load_wt, load_wp, load_pos = loads

    barrier = pltpu.get_barrier_semaphore()

    def greet_xy(d, carry):
        pl.semaphore_signal(barrier, inc=1, device_id=xy_partner(d)[1], device_id_type=MESH)
        return carry

    def greet_z(d, carry):
        pl.semaphore_signal(barrier, inc=1, device_id=z_partner(d)[1], device_id_type=MESH)
        return carry

    lax.fori_loop(1, n_xy, greet_xy, 0)
    lax.fori_loop(1, n_z, greet_z, 0)
    pl.semaphore_signal(barrier, inc=1, device_id=sibling, device_id_type=MESH)

    row_id = lax.broadcasted_iota(jnp.int32, (rows, chan), 0)
    inside = (row_id % LINE) < side
    low_mask = jnp.where(tm > 0, 1.0, 0.0).astype(F32)
    high_mask = jnp.where(tm < n_tm - 1, 1.0, 0.0).astype(F32)
    full = LINE * (side + 2)

    def shifted(ref, f):
        flat = ref[1, f].reshape(full, chan).astype(F32)
        ahead = pltpu.roll(flat, 1, 0).astype(BF16).reshape(side + 2, LINE, chan)
        behind = pltpu.roll(flat, full - 1, 0).astype(BF16).reshape(side + 2, LINE, chan)
        return ahead, behind

    def window(f):
        xs_ref[1, f] = jnp.zeros((side + 2, LINE, chan), BF16)
        xs_ref[1, f, 1 : side + 1, 0:side, :] = x_ref[0, f]
        ahead, behind = shifted(xs_ref, f)
        xs_ref[0, f] = ahead
        xs_ref[2, f] = behind

    def conv(f):
        windows = [xs_ref[b, f, a : a + side].reshape(rows, chan) for a in range(3) for b in range(3)]
        total = dot(jnp.concatenate(windows, axis=1), ws_ref[...].reshape(9 * chan, chan))
        pre_ref[f] = total
        act_ref[f + 1] = jnp.where(inside, total * sigmoid(total), 0.0).astype(BF16)

    left = (wide, (tm + n_tm - 1) % n_tm)
    right = (wide, (tm + 1) % n_tm)

    load_x.wait()
    window(0)
    window(frames - 1)
    load_ws.wait()
    conv(0)
    conv(frames - 1)
    pl.semaphore_wait(barrier, n_xy - 1 + n_z - 1 + 1)
    to_left = send(act_ref.at[1], act_ref.at[frames + 1], HALO + 1, left)
    to_right = send(act_ref.at[frames], act_ref.at[0], HALO, right)
    for f in range(1, frames - 1):
        window(f)
        conv(f)

    pooled8 = jnp.zeros((8, chan), F32)
    for f in range(frames):
        pooled8 = pooled8 + jnp.sum(
            xs_ref[1, f, 1 : side + 1].reshape(rows // 8, 8, chan).astype(F32), axis=0
        )
    load_wt.wait()
    for f in list(range(1, frames - 1)) + [0, frames - 1]:
        if f == 0:
            to_right.wait_recv()
        if f == frames - 1:
            to_left.wait_recv()
        below = dot(act_ref[f], wt_ref[0])
        above = dot(act_ref[f + 2], wt_ref[2])
        if f == 0:
            below = below * low_mask
        if f == frames - 1:
            above = above * high_mask
        pre = below + dot(act_ref[f + 1], wt_ref[1]) + above
        sig = sigmoid(pre)
        pooled8 = pooled8 + jnp.sum((pre * sig).reshape(rows // 8, 8, chan), axis=0)
        dt_ref[f] = jnp.where(inside, sig * (1.0 + pre * (1.0 - sig)), 0.0)
    pool_ref[tm] = pooled8

    def tm_partner(d):
        return (wide, (tm + d) % n_tm)

    def send_pool(d, carry):
        send(pool_ref.at[tm], pool_ref.at[tm], POOL, tm_partner(d))
        return carry

    lax.fori_loop(1, n_tm, send_pool, 0)

    dsend_ref[0] = dt_ref[0].astype(BF16)
    dsend_ref[1] = dt_ref[frames - 1].astype(BF16)
    d_left = send(dsend_ref.at[0], dhalo_ref.at[1], DHALO + 1, left)
    d_right = send(dsend_ref.at[1], dhalo_ref.at[0], DHALO, right)
    for f in range(frames):
        actt_ref[:, f * rows : (f + 1) * rows] = act_ref[f + 1].T
        for b in range(3):
            gs_ref[b, f, 0] = jnp.zeros((LINE, chan), BF16)
            gs_ref[b, f, side + 1] = jnp.zeros((LINE, chan), BF16)
    for t in range(3):
        wtt_ref[t] = wt_ref[t].T
    load_pr.wait()
    p32 = pr_ref[...].astype(F32)
    pnorm = jnp.sqrt(jnp.sum(p32 * p32, axis=1, keepdims=True) + 1e-06)
    ph_ref[...] = p32 / pnorm
    load_wp.wait()
    load_pos.wait()
    wp = wp_ref[...].astype(F32)
    ids = lax.broadcasted_iota(jnp.int32, (shard, 1), 0) + tm * shard
    multi = jnp.zeros((shard, 1), F32)
    for k in range(pos_ref.shape[1]):
        multi = multi + jnp.where(ids == pos_ref[0:1, k : k + 1], 1.0, 0.0)

    drain(pool_ref.at[0 : n_tm - 1], rcv.at[POOL])
    pooled = jnp.sum(jnp.sum(pool_ref[...], axis=0), axis=0, keepdims=True)
    zrow = jnp.sum(wp * to_column(pooled), axis=0, keepdims=True)
    znorm = jnp.sqrt(jnp.sum(zrow * zrow, axis=1, keepdims=True) + 1e-06)
    zhat = zrow / znorm
    expo = jnp.exp(16.0 * jnp.sum(ph_ref[...] * zhat, axis=1, keepdims=True))
    hits = multi * expo
    part_a = jnp.sum(ph_ref[...] * expo, axis=0, keepdims=True)
    part_b = jnp.sum(ph_ref[...] * hits, axis=0, keepdims=True)
    tiles = embed // 128
    for k in range(tiles):
        ab_ref[tm, 0, k : k + 1, :] = part_a[:, 128 * k : 128 * (k + 1)]
        ab_ref[tm, 0, tiles + k : tiles + k + 1, :] = part_b[:, 128 * k : 128 * (k + 1)]
    ab_ref[tm, 1, 0:4, :] = jnp.broadcast_to(jnp.sum(expo, axis=0, keepdims=True), (4, 128))
    ab_ref[tm, 1, 4:8, :] = jnp.broadcast_to(jnp.sum(hits, axis=0, keepdims=True), (4, 128))

    def send_ab(d, carry):
        send(ab_ref.at[tm], ab_ref.at[tm], AB, tm_partner(d))
        return carry

    lax.fori_loop(1, n_tm, send_ab, 0)
    for f in range(frames):
        pre_ref[f] = dsilu(pre_ref[f])
        xt_ref[:, f * rows : (f + 1) * rows] = xs_ref[1, f, 1 : side + 1].reshape(rows, chan).T
    drain(ab_ref.at[0 : n_tm - 1], rcv.at[AB])
    summed = jnp.sum(ab_ref[...], axis=0)
    sum_a = jnp.concatenate([summed[0, k : k + 1] for k in range(tiles)], axis=1)
    sum_b = jnp.concatenate([summed[0, tiles + k : tiles + k + 1] for k in range(tiles)], axis=1)
    total = summed[1, 0:1, 0:1]
    pos_total = summed[1, 4:5, 0:1]
    g_zhat = 16.0 * (sum_a / total - sum_b / pos_total)
    g_z = (g_zhat - zhat * jnp.sum(zhat * g_zhat, axis=1, keepdims=True)) / znorm
    g_pooled = to_row(jnp.sum(wp * g_z, axis=1, keepdims=True))
    g_s = expo / total - hits / pos_total

    for k in range(chan // 128):
        wg_ref[wide, k : k + 1, :] = pooled[:, 128 * k : 128 * (k + 1)]
    for k in range(tiles):
        wg_ref[wide, 2 + k : 3 + k, :] = g_z[:, 128 * k : 128 * (k + 1)]
        wg_ref[wide, 6 + k : 7 + k, :] = zhat[:, 128 * k : 128 * (k + 1)]
        wg_ref[wide, 10 + k : 11 + k, :] = to_row(g_s[128 * k : 128 * (k + 1)])
    wg_ref[wide, 14:16, :] = jnp.zeros((2, 128), F32)
    head_copy = send(wg_ref.at[wide], wg_ref.at[wide], HEAD, sibling)

    for f in range(frames):
        gt_ref[f + 1] = (dt_ref[f] * g_pooled).astype(BF16)
    d_right.wait_recv()
    d_left.wait_recv()
    gt_ref[0] = (dhalo_ref[0].astype(F32) * (g_pooled * low_mask)).astype(BF16)
    gt_ref[frames + 1] = (dhalo_ref[1].astype(F32) * (g_pooled * high_mask)).astype(BF16)

    half = chan // 2
    core_copies = []

    def put(q, grad):
        g, t = q // TAPS, q % TAPS
        gbuf_ref[g, 0, t] = grad[:half]
        gbuf_ref[g, 1, t] = grad[half:]

    def send_core(g):
        core_copies.append(send(gbuf_ref.at[g, 1 - core], rbuf_ref.at[g], CORE + g, sibling))

    def send_xy(g):
        core_copies[g].wait_recv()
        for t in range(TAPS):
            both = (gbuf_ref[g, core, t] + rbuf_ref[g, t]).astype(BF16)
            for p in range(n_xy):
                i, j = p // 2, p % 2
                cs_ref[g, p, t] = both[16 * i : 16 * (i + 1), 128 * j : 128 * (j + 1)]

        def one(d, carry):
            p, device = xy_partner(d)
            send(cs_ref.at[g, p], xyr_ref.at[g, d - 1], XY + g, device)
            return carry

        lax.fori_loop(1, n_xy, one, 0)

    def put_spatial(q):
        a, b = (q - 3) // 3, (q - 3) % 3
        put(q, dot(xt_ref[...], gs_ref[b, :, 2 - a : 2 - a + side].reshape(frames * rows, chan)))

    def sum_z(g):
        drain(xyr_ref.at[g], rcv.at[XY + g])
        value = cs_ref[g, mine].astype(F32)
        for d in range(n_xy - 1):
            value = value + xyr_ref[g, d].astype(F32)
        for t in range(TAPS):
            zsrc_ref[g, 2 * t] = value[t, :8]
            zsrc_ref[g, 2 * t + 1] = value[t, 8:]

        def one(d, carry):
            pz, device = z_partner(d)
            send(zsrc_ref.at[g, pz], zr_ref.at[g, d - 1], ZSUM + g, device)
            return carry

        lax.fori_loop(1, n_z, one, 0)

    def gather_z(g):
        drain(zr_ref.at[g], rcv.at[ZSUM + g])
        reduced = zsrc_ref[g, z] + jnp.sum(zr_ref[g], axis=0)
        zred_ref[g] = reduced
        zg_ref[g, z] = reduced

        def one(d, carry):
            send(zred_ref.at[g], zg_ref.at[g, z], ZALL + g, z_partner(d)[1])
            return carry

        lax.fori_loop(1, n_z, one, 0)

    def gather_xy(g):
        drain(zg_ref.at[g, 0 : n_z - 1], rcv.at[ZALL + g])
        for t in range(TAPS):
            ag_ref[g, core, mine, t] = jnp.concatenate([zg_ref[g, 2 * t], zg_ref[g, 2 * t + 1]], axis=0).astype(BF16)
        own_piece = ag_ref.at[g, core, mine]
        for dx in (2, 1, 3, 0):

            def one(dy, carry):
                send(own_piece, own_piece, XYALL + n_x * g + dx, xy_partner(dx * n_y + dy)[1])
                return carry

            lax.fori_loop(1 if dx == 0 else 0, n_y, one, 0)

    last = []

    def gather_core(g):
        for dx in (0, 1, 3, 2):
            count = n_y - 1 if dx == 0 else n_y
            drain(ag_ref.at[g, 0, 0:count], rcv.at[XYALL + n_x * g + dx])
            column = ag_ref.at[g, core, pl.ds(((x + n_x - dx) % n_x) * n_y, n_y)]
            last.append(send(column, column, COREALL + n_x * g + dx, sibling))

    for t in range(3):
        put(t, dot(actt_ref[...], gt_ref[2 - t : 2 - t + frames].reshape(frames * rows, chan)))

    for f in range(frames):
        near = jnp.concatenate([gt_ref[f + 2 - t] for t in range(3)], axis=1)
        g_act = dot(near, wtt_ref[...].reshape(3 * chan, chan))
        gs_ref[1, f, 1 : side + 1] = (g_act * pre_ref[f]).astype(BF16).reshape(side, LINE, chan)
        ahead, behind = shifted(gs_ref, f)
        gs_ref[2, f] = ahead
        gs_ref[0, f] = behind
    put_spatial(3)
    send_core(0)
    head_copy.wait_recv()
    pair_rows = wg_ref.at[pl.ds(wide - core, CORES)]
    pair_copy = send(pair_rows, pair_rows, PAIR, pair)

    for q in range(TAPS, 2 * TAPS):
        put_spatial(q)
    send_core(1)
    send_xy(0)
    pair_copy.wait_recv()
    z_rows = wg_ref.at[pl.ds(z * (CORES * X_LO), CORES * X_LO)]

    def send_head(d, carry):
        send(z_rows, z_rows, ZHEAD, z_partner(d)[1])
        return carry

    lax.fori_loop(1, n_z, send_head, 0)
    for q in range(2 * TAPS, 3 * TAPS):
        put_spatial(q)
    send_core(2)
    send_xy(1)
    send_xy(2)
    sum_z(0)

    drain(wg_ref.at[0 : n_wide - CORES * X_LO], rcv.at[ZHEAD])

    def all_clips(first, count):
        return jnp.concatenate([wg_ref[:, first + k, :] for k in range(count)], axis=1)

    over_clips = (((0,), (0,)), ((), ()))
    pooled_all = all_clips(0, chan // 128)
    g_z_all = all_clips(2, tiles)
    zhat_all = all_clips(6, tiles)
    g_s_all = all_clips(10, shard // 128)
    gproj_ref[...] = lax.dot_general(pooled_all, g_z_all, over_clips, precision=HI, preferred_element_type=F32)
    sum_z(1)
    g_phat = 16.0 * lax.dot_general(g_s_all, zhat_all, over_clips, precision=HI, preferred_element_type=F32)
    phat = ph_ref[...]
    p32 = pr_ref[...].astype(F32)
    pnorm = jnp.sqrt(jnp.sum(p32 * p32, axis=1, keepdims=True) + 1e-06)
    gprm_ref[...] = (g_phat - phat * jnp.sum(phat * g_phat, axis=1, keepdims=True)) / pnorm
    results = [
        pltpu.make_async_copy(gproj_ref, gproj_hbm, out.at[GROUPS]),
        pltpu.make_async_copy(gprm_ref, gprm_hbm, out.at[GROUPS + 1]),
    ]
    for result in results:
        result.start()

    def put_out(g):
        for copy in last[n_x * g : n_x * (g + 1)]:
            copy.wait_recv()
        result = pltpu.make_async_copy(ag_ref.at[g], ag_hbm.at[g], out.at[g])
        result.start()
        results.append(result)

    gather_z(0)
    sum_z(2)
    gather_z(1)
    gather_xy(0)
    gather_z(2)
    gather_xy(1)
    gather_core(0)
    gather_xy(2)
    gather_core(1)
    put_out(0)
    gather_core(2)
    put_out(1)
    put_out(2)

    for copy in [to_left, to_right, d_left, d_right, head_copy, pair_copy] + core_copies + last:
        copy.wait_send()
    drain(pool_ref.at[0 : n_tm - 1], snd.at[POOL])
    drain(ab_ref.at[0 : n_tm - 1], snd.at[AB])
    drain(wg_ref.at[0 : n_wide - CORES * X_LO], snd.at[ZHEAD])
    for g in range(GROUPS):
        drain(xyr_ref.at[g], snd.at[XY + g])
        drain(zr_ref.at[g], snd.at[ZSUM + g])
        drain(zg_ref.at[g, 0 : n_z - 1], snd.at[ZALL + g])
        for dx in range(n_x):
            drain(ag_ref.at[g, 0, 0 : n_y - 1 if dx == 0 else n_y], snd.at[XYALL + n_x * g + dx])
    for result in results:
        result.wait()


def lay_kernel(
    ag_hbm, gproj_hbm, gprm_hbm, gs_out, gt_out, gproj_out, gprm_out,
    ag_ref, gproj_ref, gprm_ref, buf_ref, load_sems, sems,
):
    groups, cores, pieces, taps = ag_ref.shape[:4]
    loads = [pltpu.make_async_copy(ag_hbm.at[g], ag_ref.at[g], load_sems.at[g]) for g in range(groups)]
    loads.append(pltpu.make_async_copy(gprm_hbm, gprm_ref, load_sems.at[groups]))
    loads.append(pltpu.make_async_copy(gproj_hbm, gproj_ref, load_sems.at[groups + 1]))
    for load in loads:
        load.start()
    copies = []
    half = buf_ref.shape[1] // cores
    for q in range(groups * taps):
        if q % taps == 0:
            loads[q // taps].wait()
        for c in range(cores):
            for p in range(pieces):
                i, j = p // 2, p % 2
                r = half * c + 16 * i
                buf_ref[q, r : r + 16, 128 * j : 128 * (j + 1)] = ag_ref[q // taps, c, p, q % taps].astype(F32)
        target = gt_out.at[q] if q < 3 else gs_out.at[q - 3]
        copies.append(pltpu.make_async_copy(buf_ref.at[q], target, sems.at[q]))
        copies[-1].start()
    loads[groups].wait()
    copies.append(pltpu.make_async_copy(gprm_ref, gprm_out, sems.at[12]))
    copies[-1].start()
    loads[groups + 1].wait()
    copies.append(pltpu.make_async_copy(gproj_ref, gproj_out, sems.at[13]))
    copies[-1].start()
    for copy in copies:
        copy.wait()


def body(clips_in, w_spatial, w_temporal, w_proj, prompts, positives):
    n_wide, n_tm = lax.axis_size("wide"), lax.axis_size("tm")
    clips, frames, side, _, chan = clips_in.shape
    shard, embed = prompts.shape
    rows = side * LINE
    n_z = n_wide // (X_LO * CORES)
    n_xy = X_HI * X_LO * (n_tm // X_HI)
    sizes = (n_wide, n_tm, frames, side, chan, embed, shard)
    hbm = pl.BlockSpec(memory_space=pltpu.HBM)
    half = chan // 2
    gathered, grad_proj, grad_prompts = pl.pallas_call(
        functools.partial(step_kernel, sizes),
        out_shape=(
            jax.ShapeDtypeStruct((GROUPS, CORES, n_xy, TAPS, 16, 128), BF16),
            jax.ShapeDtypeStruct((chan, embed), F32),
            jax.ShapeDtypeStruct((shard, embed), F32),
        ),
        in_specs=[hbm] * 6,
        out_specs=(hbm,) * 3,
        scratch_shapes=[
            pltpu.VMEM((3, frames, side + 2, LINE, chan), BF16),
            pltpu.VMEM((frames, rows, chan), F32),
            pltpu.VMEM((frames + 2, rows, chan), BF16),
            pltpu.VMEM((frames, rows, chan), F32),
            pltpu.VMEM((2, rows, chan), BF16),
            pltpu.VMEM((2, rows, chan), BF16),
            pltpu.VMEM((frames + 2, rows, chan), BF16),
            pltpu.VMEM((3, frames, side + 2, LINE, chan), BF16),
            pltpu.VMEM((chan, frames * rows), BF16),
            pltpu.VMEM((chan, frames * rows), BF16),
            pltpu.VMEM((3, chan, chan), BF16),
            pltpu.VMEM((shard, embed), F32),
            pltpu.VMEM((n_tm, 8, chan), F32),
            pltpu.VMEM((n_tm, 2, 8, 128), F32),
            pltpu.VMEM((n_wide, 16, 128), F32),
            pltpu.VMEM((GROUPS, 2, TAPS, half, chan), F32),
            pltpu.VMEM((GROUPS, TAPS, half, chan), F32),
            pltpu.VMEM((GROUPS, n_xy, TAPS, 16, 128), BF16),
            pltpu.VMEM((GROUPS, n_xy - 1, TAPS, 16, 128), BF16),
            pltpu.VMEM((GROUPS, n_z, 8, 128), F32),
            pltpu.VMEM((GROUPS, n_z - 1, 8, 128), F32),
            pltpu.VMEM((GROUPS, 8, 128), F32),
            pltpu.VMEM((GROUPS, n_z, 8, 128), F32),
            pltpu.VMEM((9, chan, chan), BF16),
            pltpu.VMEM((3, chan, chan), BF16),
            pltpu.VMEM((chan, embed), BF16),
            pltpu.VMEM((shard, embed), BF16),
            pltpu.VMEM(positives.shape, jnp.int32),
            pltpu.VMEM(clips_in.shape, BF16),
            pltpu.VMEM((GROUPS, CORES, n_xy, TAPS, 16, 128), BF16),
            pltpu.VMEM((chan, embed), F32),
            pltpu.VMEM((shard, embed), F32),
            pltpu.SemaphoreType.DMA((SEMS,)),
            pltpu.SemaphoreType.DMA((SEMS,)),
            pltpu.SemaphoreType.DMA((6,)),
            pltpu.SemaphoreType.DMA((GROUPS + 2,)),
        ],
        compiler_params=pltpu.CompilerParams(
            collective_id=0, has_side_effects=True, vmem_limit_bytes=66_500_000
        ),
        name="step",
    )(clips_in, w_spatial.reshape(9, chan, chan), w_temporal, w_proj, prompts, positives)
    grad_s, grad_t, grad_p, grad_m = pl.pallas_call(
        lay_kernel,
        out_shape=(
            jax.ShapeDtypeStruct((9, chan, chan), F32),
            jax.ShapeDtypeStruct((3, chan, chan), F32),
            jax.ShapeDtypeStruct((chan, embed), F32),
            jax.ShapeDtypeStruct((shard, embed), F32),
        ),
        in_specs=[hbm] * 3,
        out_specs=(hbm,) * 4,
        scratch_shapes=[
            pltpu.VMEM((GROUPS, CORES, n_xy, TAPS, 16, 128), BF16),
            pltpu.VMEM((chan, embed), F32),
            pltpu.VMEM((shard, embed), F32),
            pltpu.VMEM((12, chan, chan), F32),
            pltpu.SemaphoreType.DMA((GROUPS + 2,)),
            pltpu.SemaphoreType.DMA((14,)),
        ],
        compiler_params=pltpu.CompilerParams(vmem_limit_bytes=66_500_000),
        name="lay_out",
    )(gathered, grad_proj, grad_prompts)
    return grad_s.reshape(3, 3, chan, chan), grad_t, grad_p, grad_m


def solution(mesh):
    placed = (P("wide", "tm", None, None, None), P(), P(), P(), P("tm", None), P("wide", None))
    return jax.shard_map(
        body, mesh=mesh, in_specs=placed, out_specs=(P(), P(), P(), P("tm", None)), check_vma=False
    )
```
